32 devices in a mesh: tm: 2 (over x), height: 4 (over z), head: 4 (over y, core).
Axes of the slice: x: 2, y: 2, z: 4, core: 2. Of those that a mesh axis runs over, the one named last changes fastest.
Arguments:
- query_in: bfloat16 [12, 8, 32, 16, 128], P('head', 'tm', 'height'), may hold values from -8 to 8
- key_in: bfloat16 [12, 8, 32, 16, 128], P('head', 'tm', 'height'), may hold values from -8 to 8
- value_in: bfloat16 [12, 8, 32, 16, 128], P('head', 'tm', 'height'), may hold values from -6 to 6
- out_grad: bfloat16 [12, 8, 32, 16, 128], P('head', 'tm', 'height'), may hold values from -6 to 6
Outputs:
- query_grad: bfloat16 [12, 8, 32, 16, 128], P('head', 'tm', 'height')
- key_grad: bfloat16 [12, 8, 32, 16, 128], P('head', 'tm', 'height')
- value_grad: bfloat16 [12, 8, 32, 16, 128], P('head', 'tm', 'height')
The draws below stay inside these ranges and needn't reach their ends.
All inputs are finite; a program needn't handle non-finite values.
Results may differ from the reference program's by a relative error of at most 0.0093.
Values may be sent and summed in bfloat16 or wider, within the bound.
A program may use at most 128 MiB of HBM per device.

```python
import jax
import jax.numpy as jnp
from jax import lax

HEADS = 12
HEAD_DIM = 128
TILE_F = 4
TILE_R = 8
TILE_C = 8
COLS = 16
NF = 8
NR = 32


def draw_pair(key):
    full_shape = (HEADS, NF, NR, COLS, HEAD_DIM)
    seed_list = jax.random.split(jax.random.fold_in(key, 41), 2)
    query_draw = jax.random.truncated_normal(seed_list[0], -4.0, 4.0, full_shape, jnp.float32)
    key_draw = jax.random.truncated_normal(seed_list[1], -4.0, 4.0, full_shape, jnp.float32)
    return (query_draw, key_draw)


def draw_query_in(key, part):
    return draw_pair(key)[0].astype(jnp.bfloat16)


def draw_key_in(key, part):
    return draw_pair(key)[1].astype(jnp.bfloat16)


def levels(rng, shape, pieces, least, high):
    def one(axis_at, blocks):
        draws = jax.random.uniform(jax.random.fold_in(jax.random.fold_in(rng, 6), axis_at), (blocks,), jnp.float32, least / len(pieces), high / len(pieces))
        return jnp.repeat(jnp.exp(draws), shape[axis_at] // blocks).reshape((-1,) + (1,) * (len(shape) - axis_at - 1))

    factor_of = one(*pieces[0])
    for cut in pieces[1:]:
        factor_of = factor_of * one(*cut)
    return factor_of


def centred(own_key, shape, scale, reach, pieces=(), held_as=jnp.bfloat16):
    level = levels(own_key, shape, pieces, -0.22, 0.18) if pieces else 1.0
    array = jax.random.normal(own_key, shape, jnp.float32) * scale * level
    return jnp.minimum(jnp.maximum(array, -reach), reach).astype(held_as)


def setup_inputs(seed: int = 0) -> dict:
    keys = jax.random.split(jax.random.key(seed), 5)
    return {
        "query_in": draw_query_in(jax.random.fold_in(keys[4], 71), 0),
        "key_in": draw_key_in(jax.random.fold_in(keys[4], 71), 0),
        "value_in": centred(keys[2], (HEADS, NF, NR, COLS, HEAD_DIM), 1.0, 6.0, ((0, 4), (1, 2), (2, 4))),
        "out_grad": centred(keys[3], (HEADS, NF, NR, COLS, HEAD_DIM), 1.0, 6.0, ((0, 4), (1, 2), (2, 4))),
    }


def rounded(values):
    return lax.optimization_barrier(values.astype(jnp.bfloat16)).astype(jnp.float32)


def batched(form, left_op, right_op):
    return jnp.einsum(form, left_op.astype(jnp.float32), right_op.astype(jnp.float32))


def corner_at(first, second, third, rank):
    anchor = jnp.zeros((), jnp.int32)
    middle = (first.astype(jnp.int32), second.astype(jnp.int32), third.astype(jnp.int32))
    return (anchor,) + middle + (anchor,) * (rank - 4)


def tiles_back(stacked, grid_f, grid_r, grid_c):
    head_count, tile_f, tile_r, tile_c = stacked.shape[1:5]
    trailing = stacked.shape[5:]
    split = stacked.reshape((grid_f, grid_r, grid_c, head_count, tile_f, tile_r, tile_c) + trailing)
    order = (3, 0, 4, 1, 5, 2, 6) + tuple(range(7, 7 + len(trailing)))
    return split.transpose(order).reshape((head_count, grid_f * tile_f, grid_r * tile_r, grid_c * tile_c) + trailing)


def reference(query_in, key_in, value_in, out_grad):
    head_count, frame_count, row_count, col_count, head_depth = query_in.shape
    score_scale = head_depth ** -0.5
    grid_f = frame_count // TILE_F
    grid_r = row_count // TILE_R
    grid_c = col_count // TILE_C
    border = ((0, 0), (TILE_F, TILE_F), (TILE_R, TILE_R), (TILE_C, TILE_C), (0, 0))
    inside = jnp.pad(jnp.ones((1, frame_count, row_count, col_count, 1), jnp.float32), border)
    tile_shape = (head_count, TILE_F, TILE_R, TILE_C, head_depth)
    span_shape = (head_count, 3 * TILE_F, 3 * TILE_R, 3 * TILE_C, head_depth)
    mask_shape = (1, 3 * TILE_F, 3 * TILE_R, 3 * TILE_C, 1)
    stat_tile = tile_shape[:4]
    stat_span = span_shape[:4]
    key_pad = jnp.pad(key_in, border)
    value_pad = jnp.pad(value_in, border)

    def tile_place(tile_index):
        first = tile_index // (grid_r * grid_c)
        second = (tile_index // grid_c) % grid_r
        third = tile_index % grid_c
        return first * TILE_F, second * TILE_R, third * TILE_C

    def query_tile(tile_index):
        first, second, third = tile_place(tile_index)
        corner = corner_at(first, second, third, 5)
        q_rows = lax.dynamic_slice(query_in, corner, tile_shape).reshape(head_count, -1, head_depth)
        g_rows = lax.dynamic_slice(out_grad, corner, tile_shape).reshape(head_count, -1, head_depth)
        k_span = lax.dynamic_slice(key_pad, corner, span_shape).reshape(head_count, -1, head_depth)
        v_span = lax.dynamic_slice(value_pad, corner, span_shape).reshape(head_count, -1, head_depth)
        live_mask = lax.dynamic_slice(inside, corner, mask_shape).reshape(1, 1, -1) > 0.5
        scores = jnp.where(live_mask, batched("hqd,hkd->hqk", q_rows, k_span) * score_scale, -jnp.inf)
        row_max = jnp.max(scores, axis=-1, keepdims=True)
        log_total = row_max + jnp.log(jnp.sum(jnp.exp(scores - row_max), axis=-1, keepdims=True))
        weights = jnp.exp(scores - log_total)
        weight_bf = rounded(weights)
        attended = batched("hqk,hkd->hqd", weight_bf, v_span)
        row_delta = jnp.sum(g_rows.astype(jnp.float32) * attended, axis=-1, keepdims=True)
        d_weights = batched("hqd,hkd->hqk", g_rows, v_span)
        d_scores = rounded(weights * (d_weights - row_delta))
        grad_rows = batched("hqk,hkd->hqd", d_scores, k_span) * score_scale
        return (grad_rows.astype(jnp.bfloat16).reshape(tile_shape), log_total.reshape(stat_tile), row_delta.reshape(stat_tile))

    tile_ids = jnp.arange(grid_f * grid_r * grid_c, dtype=jnp.int32)
    grad_tiles, total_tiles, delta_tiles = lax.map(query_tile, tile_ids)
    query_grad = tiles_back(grad_tiles, grid_f, grid_r, grid_c)
    log_totals = tiles_back(total_tiles, grid_f, grid_r, grid_c)
    deltas = tiles_back(delta_tiles, grid_f, grid_r, grid_c)
    query_pad = jnp.pad(query_in, border)
    grad_pad = jnp.pad(out_grad, border)
    total_pad = jnp.pad(log_totals, border[:4])
    delta_pad = jnp.pad(deltas, border[:4])

    def key_tile(tile_index):
        first, second, third = tile_place(tile_index)
        corner = corner_at(first, second, third, 5)
        corner_stat = corner_at(first, second, third, 4)
        k_rows = lax.dynamic_slice(key_in, corner, tile_shape).reshape(head_count, -1, head_depth)
        v_rows = lax.dynamic_slice(value_in, corner, tile_shape).reshape(head_count, -1, head_depth)
        q_span = lax.dynamic_slice(query_pad, corner, span_shape).reshape(head_count, -1, head_depth)
        g_span = lax.dynamic_slice(grad_pad, corner, span_shape).reshape(head_count, -1, head_depth)
        total_span = lax.dynamic_slice(total_pad, corner_stat, stat_span).reshape(head_count, -1, 1)
        delta_span = lax.dynamic_slice(delta_pad, corner_stat, stat_span).reshape(head_count, -1, 1)
        live_mask = lax.dynamic_slice(inside, corner, mask_shape).reshape(1, -1, 1) > 0.5
        scores = jnp.where(live_mask, batched("hqd,hkd->hqk", q_span, k_rows) * score_scale, -jnp.inf)
        weights = jnp.exp(scores - total_span)
        weight_bf = rounded(weights)
        d_weights = batched("hqd,hkd->hqk", g_span, v_rows)
        d_scores = rounded(weights * (d_weights - delta_span))
        key_part = batched("hqk,hqd->hkd", d_scores, q_span) * score_scale
        value_part = batched("hqk,hqd->hkd", weight_bf, g_span)
        return (key_part.astype(jnp.bfloat16).reshape(tile_shape), value_part.astype(jnp.bfloat16).reshape(tile_shape))

    key_tiles, value_tiles = lax.map(key_tile, tile_ids)
    key_grad = tiles_back(key_tiles, grid_f, grid_r, grid_c)
    value_grad = tiles_back(value_tiles, grid_f, grid_r, grid_c)
    return query_grad, key_grad, value_grad
```

```python
import jax
import jax.numpy as jnp
from jax import lax
from jax.experimental import pallas as pl
from jax.experimental.pallas import tpu as pltpu
from jax.sharding import PartitionSpec as P

TILE_C = 8


def shifted(block, axis, distance):
    devices = range(lax.axis_size(axis))
    route = [(i - distance, i) for i in devices if i - distance in devices]
    return lax.ppermute(block, axis, route)


def shortened(x):
    return jax.tree.map(lambda a: a.astype(jnp.bfloat16) if a.dtype == jnp.float32 else a, x)


def extended(x, sides, width):
    for axis, dim in sides:
        size, length = (lax.axis_size(axis), x.shape[dim])
        up = [(i, (i + 1) % size) for i in range(size - 1)]
        down = [(j, i) for i, j in up]
        last = lax.slice_in_dim(x, length - width, length, axis=dim)
        first = lax.slice_in_dim(x, 0, width, axis=dim)
        before = lax.ppermute(last, axis, up)
        after = lax.ppermute(first, axis, down)
        x = jnp.concatenate([before, x, after], axis=dim)
    return x


def neighbour_live():
    offsets = jnp.arange(3, dtype=jnp.int32) - 1
    frame_pos = lax.axis_index("tm") + offsets
    row_pos = lax.axis_index("height") + offsets
    frame_ok = (frame_pos >= 0) & (frame_pos < lax.axis_size("tm"))
    row_ok = (row_pos >= 0) & (row_pos < lax.axis_size("height"))
    return frame_ok[:, None] & row_ok[None, :]


def span_live(neighbour_ok, tile_index, span_start, frame_count, row_count, span_width, col_tile):
    columns = span_start + jnp.arange(span_width, dtype=jnp.int32)
    near_cols = jnp.abs(columns // col_tile - tile_index) <= 1
    live_mask = neighbour_ok[:, :, None, None, None] & near_cols[None, None, None, None, :]
    return jnp.broadcast_to(live_mask, (3, 3, frame_count, row_count, span_width)).reshape(-1)


def scores_of(left_rows, right_rows, live_mask, score_scale):
    raw_scores = (
        jnp.einsum("hqd,hkd->hqk", left_rows, right_rows, preferred_element_type=jnp.float32)
        * score_scale
    )
    return jnp.where(live_mask, raw_scores, -jnp.inf)


def whole_span(array, span_start, span_size, axis_pos):
    return isinstance(span_start, int) and span_start == 0 and (span_size == array.shape[axis_pos])


def cut_span(array, span_start, span_size, axis_pos):
    if whole_span(array, span_start, span_size, axis_pos):
        return array
    return lax.dynamic_slice_in_dim(array, jnp.asarray(span_start, jnp.int32), span_size, axis_pos)


def add_span(array, piece):
    return array + piece


def run_tiles(tile_step, tile_count, col_tile, carried):
    edge_width = 2 * col_tile
    carried = tile_step(0, 0, edge_width, carried)
    return tile_step(tile_count - 1, (tile_count - 2) * col_tile, edge_width, carried)


def send_rows(parts, offset):
    return (
        shifted(parts[0].astype(jnp.bfloat16), "height", offset).astype(jnp.float32),
        shifted(parts[1].astype(jnp.bfloat16), "height", offset).astype(jnp.float32),
    )


def send_frames(parts, offset):
    return shifted((shortened(parts[0]), shortened(parts[1])), "tm", offset)


def local(query_in, key_in, value_in, out_grad):
    head_count, frame_count, row_count, col_count, head_depth = query_in.shape
    col_tile = TILE_C
    tile_count = col_count // col_tile
    score_scale = head_depth ** (-0.5)
    spread_shape = (head_count, 1, 1, frame_count, row_count, col_count, head_depth)
    ext_shape = (head_count, 3, 3, frame_count, row_count, col_count, head_depth)
    stat_shape = (head_count, frame_count, row_count, col_tile)
    neighbour_ok = neighbour_live()
    keys_ext, values_ext = (
        extended(key_in.reshape(spread_shape), (("tm", 1), ("height", 2)), 1),
        extended(value_in.reshape(spread_shape), (("tm", 1), ("height", 2)), 1),
    )

    def query_step(tile_index, span_start, span_width, carried):
        grad_q, row_totals, row_deltas, grad_k, grad_v = carried
        own_start = jnp.asarray(tile_index * col_tile, jnp.int32)
        q_rows = cut_span(query_in, own_start, col_tile, 3).reshape(head_count, -1, head_depth)
        g_rows = cut_span(out_grad, own_start, col_tile, 3).reshape(head_count, -1, head_depth)
        k_span = cut_span(keys_ext, span_start, span_width, 5).reshape(head_count, -1, head_depth)
        v_span = cut_span(values_ext, span_start, span_width, 5).reshape(head_count, -1, head_depth)
        live_mask = span_live(
            neighbour_ok, tile_index, span_start, frame_count, row_count, span_width, col_tile
        )
        scores = scores_of(q_rows, k_span, live_mask[None, None, :], score_scale)
        row_max = jnp.max(scores, axis=-1, keepdims=True)
        log_total = row_max + jnp.log(jnp.sum(jnp.exp(scores - row_max), axis=-1, keepdims=True))
        weights = jnp.exp(scores - log_total)
        weight_bf = weights.astype(jnp.bfloat16)
        attended = jnp.einsum("hqk,hkd->hqd", weight_bf, v_span, preferred_element_type=jnp.float32)
        row_delta = jnp.sum(g_rows.astype(jnp.float32) * attended, axis=-1, keepdims=True)
        d_weights = jnp.einsum("hqd,hkd->hqk", g_rows, v_span, preferred_element_type=jnp.float32)
        d_scores = (weights * (d_weights - row_delta)).astype(jnp.bfloat16)
        grad_piece = (
            jnp.einsum("hqk,hkd->hqd", d_scores, k_span, preferred_element_type=jnp.float32)
            * score_scale
        )
        grad_q = lax.dynamic_update_slice_in_dim(
            grad_q, grad_piece.reshape(stat_shape + (head_depth,)), own_start, 3
        )
        row_totals = lax.dynamic_update_slice_in_dim(
            row_totals, log_total.reshape(stat_shape), own_start, 3
        )
        row_deltas = lax.dynamic_update_slice_in_dim(
            row_deltas, row_delta.reshape(stat_shape), own_start, 3
        )
        span_shape = (head_count, 3, 3, frame_count, row_count, span_width, head_depth)
        key_piece = (
            jnp.einsum("hqk,hqd->hkd", d_scores, q_rows, preferred_element_type=jnp.float32)
            * score_scale
        )
        value_piece = jnp.einsum(
            "hqk,hqd->hkd", weight_bf, g_rows, preferred_element_type=jnp.float32
        )
        grad_k = add_span(grad_k, key_piece.reshape(span_shape))
        grad_v = add_span(grad_v, value_piece.reshape(span_shape))
        return (grad_q, row_totals, row_deltas, grad_k, grad_v)

    stat_full = (head_count, frame_count, row_count, col_count)
    initial = (
        jnp.zeros(query_in.shape, jnp.float32),
        jnp.zeros(stat_full, jnp.float32),
        jnp.zeros(stat_full, jnp.float32),
        jnp.zeros(ext_shape, jnp.float32),
        jnp.zeros(ext_shape, jnp.float32),
    )
    grad_q, row_totals, row_deltas, grad_k, grad_v = run_tiles(
        query_step, tile_count, col_tile, initial
    )
    query_grad = grad_q.astype(jnp.bfloat16)
    from_above = send_rows((grad_k[:, :, 0], grad_v[:, :, 0]), -1)
    from_below = send_rows((grad_k[:, :, 2], grad_v[:, :, 2]), 1)
    part_k = grad_k[:, :, 1] + from_above[0] + from_below[0]
    part_v = grad_v[:, :, 1] + from_above[1] + from_below[1]
    from_next = send_frames((part_k[:, 0], part_v[:, 0]), -1)
    from_prev = send_frames((part_k[:, 2], part_v[:, 2]), 1)
    key_total = part_k[:, 1] + from_next[0] + from_prev[0]
    value_total = part_v[:, 1] + from_next[1] + from_prev[1]
    return (query_grad, key_total.astype(jnp.bfloat16), value_total.astype(jnp.bfloat16))


LOG2_E = 1.4426950408889634


def job_kinds(slot, slots):
    return ("keys" if slot < slots // 2 else "queries", "keys" if slot < slots - slots // 2 else "queries")


def banded_kernel(
    q_in, k_in, v_in, g_in, q_out, k_out, v_out,
    zb, xb, probs, dws, block_stats, sloc, sfar, total, fin, kacc, vacc, qacc,
    zsend, xsend, zgot, xgot,
    loc, xis, xir, zis, zir, ss, sr, xos, xor_, zos, zor,
):
    slots, tokens, depth = q_in.shape
    scale = depth ** (-0.5)
    rate = scale * LOG2_E
    f32, bf = jnp.float32, jnp.bfloat16
    x = lax.axis_index("tm")
    z = lax.axis_index("height")
    z_count = lax.axis_size("height")
    parity = lax.rem(lax.axis_index("head"), 2)
    other = 1 - x

    def at_z(distance):
        return (z + distance >= 0) & (z + distance < z_count)

    def live(i):
        return at_z(i - 1)

    def each(s, action):
        kinds = job_kinds(s, slots)
        if kinds[0] == kinds[1]:
            action(s, kinds[0])
        else:
            for p in range(2):
                @pl.when(parity == p)
                def _():
                    action(s, kinds[p])

    def x_side(kind):
        return (q_in, g_in) if kind == "queries" else (k_in, v_in)

    def z_side(kind):
        return (k_in, v_in) if kind == "queries" else (q_in, g_in)

    def key_first(kind, i, j):
        return (zb, i, xb, j) if kind == "queries" else (xb, j, zb, i)

    nothing = jnp.concatenate(
        [jnp.full((1, tokens), -jnp.inf, f32), jnp.zeros((7, tokens), f32)], axis=0
    )
    block_stats[...] = jnp.broadcast_to(nothing, block_stats.shape)
    sfar[...] = jnp.broadcast_to(nothing, sfar.shape)

    def own_copies(s, kind):
        return [
            pltpu.make_async_copy(x_side(kind)[a].at[s], xb.at[s, a, 0], loc.at[s, a, 0])
            for a in range(2)
        ] + [
            pltpu.make_async_copy(z_side(kind)[a].at[s], zb.at[s, a, 1], loc.at[s, a, 1])
            for a in range(2)
        ]

    def start_own(s, kind):
        for copy in own_copies(s, kind):
            copy.start()

    barrier = pltpu.get_barrier_semaphore()
    pl.semaphore_signal(barrier, inc=1, device_id={"tm": other})
    for distance in (-2, -1, 1, 2):
        @pl.when(at_z(distance))
        def _():
            pl.semaphore_signal(barrier, inc=1, device_id={"height": z + distance})
    for s in range(slots):
        each(s, start_own)
    pl.semaphore_wait(barrier, 1 + sum(jnp.where(at_z(n), 1, 0) for n in (-2, -1, 1, 2)))

    def x_in(s, a, kind):
        return pltpu.make_async_remote_copy(
            src_ref=x_side(kind)[a].at[s], dst_ref=xb.at[s, a, 1],
            send_sem=xis.at[s, a], recv_sem=xir.at[s, a], device_id={"tm": other},
        )

    def z_in(s, a, d, kind):
        return pltpu.make_async_remote_copy(
            src_ref=z_side(kind)[a].at[s], dst_ref=zb.at[s, a, 2 - d],
            send_sem=zis.at[s, a, d], recv_sem=zir.at[s, a, 2 - d], device_id={"height": z + d - 1},
        )

    def z_arrived(s, a, i, kind):
        return pltpu.make_async_remote_copy(
            src_ref=z_side(kind)[a].at[s], dst_ref=zb.at[s, a, i],
            send_sem=zis.at[s, a, 0], recv_sem=zir.at[s, a, i], device_id={"height": z + i - 1},
        )

    def send_in(s, a):
        def action(s, kind):
            x_in(s, a, kind).start()
            for d in (0, 2):
                @pl.when(live(d))
                def _():
                    z_in(s, a, d, kind).start()
        each(s, action)

    def folded(block):
        return block.reshape(tokens // 8, 8, tokens)

    def row(ref, n):
        return ref[n:n + 1, :]

    def score_block(s, i, j, kind, turn):
        kz, ki, qz, qi = key_first(kind, i, j)

        def arrive(a):
            @pl.when(turn == 1)
            def _():
                x_in(s, a, kind).wait_recv()

            @pl.when((turn > 1) & (j == 0))
            def _():
                z_arrived(s, a, i, kind).wait_recv()

        arrive(0)
        raw = lax.dot_general(
            kz[s, 0, ki], qz[s, 0, qi], (((1,), (1,)), ((), ())), preferred_element_type=f32
        )
        top = jnp.max(jnp.max(folded(raw), axis=0), axis=0, keepdims=True)
        arrive(1)
        dw = lax.dot_general(
            kz[s, 1, ki], qz[s, 1, qi], (((1,), (1,)), ((), ())), preferred_element_type=f32
        )
        prob = jnp.exp2((raw - top) * rate)
        probs[s, i, j] = prob
        dws[s, i, j] = dw
        out = block_stats.at[s, i, j]
        out[0:1, :] = top
        out[1:2, :] = jnp.sum(jnp.sum(folded(prob), axis=0), axis=0, keepdims=True)
        out[2:3, :] = jnp.sum(jnp.sum(folded(prob * dw), axis=0), axis=0, keepdims=True)

    def scores(s, first, last):
        def action(s, kind):
            if first == 0:
                for copy in own_copies(s, kind):
                    copy.wait()

            @pl.loop(first, last)
            def _(turn):
                i = lax.rem(1 + 2 * (turn // 2), 3)
                j = lax.rem(turn, 2)

                @pl.when(live(i))
                def _():
                    score_block(s, i, j, kind, turn)
        each(s, action)

    def merged(parts):
        top = row(parts[0], 0)
        for part in parts[1:]:
            top = jnp.maximum(top, row(part, 0))
        factors = [jnp.exp2((row(part, 0) - top) * rate) for part in parts]
        mass = sum(row(part, 1) * f for part, f in zip(parts, factors))
        pull = sum(row(part, 2) * f for part, f in zip(parts, factors))
        return top, mass, pull

    def x_stat(s, j):
        return pltpu.make_async_remote_copy(
            src_ref=sloc.at[s, j], dst_ref=sfar.at[s, 1 - j, 0],
            send_sem=ss.at[s, j, 0], recv_sem=sr.at[s, 1 - j, 0], device_id={"tm": other},
        )

    def z_stat(s, i, r):
        return pltpu.make_async_remote_copy(
            src_ref=sloc.at[s, i], dst_ref=sfar.at[s, 2 - r, 2 - i],
            send_sem=ss.at[s, i, r], recv_sem=sr.at[s, 2 - r, 2 - i],
            device_id={"height": z + i + r - 2},
        )

    def z_stat_arrived(s, i, r):
        return pltpu.make_async_remote_copy(
            src_ref=sloc.at[s, i], dst_ref=sfar.at[s, i, r],
            send_sem=ss.at[s, i, r], recv_sem=sr.at[s, i, r],
            device_id={"height": z + i + r - 2},
        )

    def for_z_stats(action):
        for i in range(3):
            for r in range(3):
                if r != 2 - i:
                    @pl.when(live(i) & at_z(i + r - 2))
                    def _():
                        action(i, r)

    def send_stats(s):
        def action(s, kind):
            if kind == "queries":
                for j in range(2):
                    for n, value in enumerate(merged([block_stats.at[s, i, j] for i in range(3)])):
                        sloc[s, j, n:n + 1, :] = value
                    x_stat(s, j).start()
            else:
                for i in range(3):
                    @pl.when(live(i))
                    def _():
                        for n, value in enumerate(merged([block_stats.at[s, i, j] for j in range(2)])):
                            sloc[s, i, n:n + 1, :] = value
                for_z_stats(lambda i, r: z_stat(s, i, r).start())
        each(s, action)

    def take_stats(s):
        def settle(b, far):
            top, mass, pull = merged([sloc.at[s, b]] + far)
            inverse = 1.0 / mass
            total[s, b, 0:1, :] = top
            total[s, b, 1:2, :] = inverse
            total[s, b, 2:3, :] = pull * inverse

        def action(s, kind):
            if kind == "queries":
                for j in range(2):
                    x_stat(s, 1 - j).wait_recv()
                    settle(j, [sfar.at[s, j, 0]])
            else:
                for_z_stats(lambda i, r: z_stat_arrived(s, i, r).wait_recv())
                for i in range(3):
                    @pl.when(live(i))
                    def _():
                        settle(i, [sfar.at[s, i, r] for r in range(3) if r != 2 - i])
        each(s, action)

    def z_out(s, a, d):
        return pltpu.make_async_remote_copy(
            src_ref=zsend.at[s, a, d // 2], dst_ref=zgot.at[s, a, 1 - d // 2],
            send_sem=zos.at[s, a, d // 2], recv_sem=zor.at[s, a, 1 - d // 2],
            device_id={"height": z + d - 1},
        )

    def z_back(s, a, d):
        return pltpu.make_async_remote_copy(
            src_ref=zsend.at[s, a, d // 2], dst_ref=zgot.at[s, a, d // 2],
            send_sem=zos.at[s, a, d // 2], recv_sem=zor.at[s, a, d // 2],
            device_id={"height": z + d - 1},
        )

    def x_out(s, a):
        return pltpu.make_async_remote_copy(
            src_ref=xsend.at[s, a], dst_ref=xgot.at[s, a],
            send_sem=xos.at[s, a], recv_sem=xor_.at[s, a], device_id={"tm": other},
        )

    def grad_block(s, i, kind):
        pieces = []
        for j in range(2):
            kz, ki, qz, qi = key_first(kind, i, j)
            goal = total.at[s, j if kind == "queries" else i]
            mass = jnp.exp2((row(block_stats.at[s, i, j], 0) - row(goal, 0)) * rate) * row(goal, 1)
            weight = probs[s, i, j] * mass
            ds = (weight * (dws[s, i, j] - row(goal, 2))).astype(bf)
            dv = jnp.dot(weight.astype(bf), qz[s, 1, qi], preferred_element_type=f32)
            dk = jnp.dot(ds, qz[s, 0, qi], preferred_element_type=f32)
            dq = lax.dot_general(
                kz[s, 0, ki], ds, (((0,), (0,)), ((), ())), preferred_element_type=f32
            )
            pieces.append((dk, dv, dq))
        if kind == "queries":
            for j in range(2):
                qacc[j] += pieces[j][2]
            done = ((pieces[0][0] + pieces[1][0]) * scale, pieces[0][1] + pieces[1][1])
            places = (1, 2)
        else:
            for j in range(2):
                kacc[j] += pieces[j][0]
                vacc[j] += pieces[j][1]
            done = ((pieces[0][2] + pieces[1][2]).T * scale,)
            places = (0,)

        @pl.when(i == 1)
        def _():
            for value, place in zip(done, places):
                fin[s, place] = value

        @pl.when(i != 1)
        def _():
            for a, value in enumerate(done):
                zsend[s, a, i // 2] = value.astype(bf)
                z_out(s, a, i).start()

    def grads(s):
        def action(s, kind):
            if kind == "queries":
                qacc[...] = jnp.zeros_like(qacc)
            else:
                kacc[...] = jnp.zeros_like(kacc)
                vacc[...] = jnp.zeros_like(vacc)

            @pl.loop(0, 3)
            def _(turn):
                i = lax.rem(2 * turn, 3)

                @pl.when(live(i))
                def _():
                    grad_block(s, i, kind)

            if kind == "queries":
                fin[s, 0] = qacc[0].T * scale
                xsend[s, 0] = (qacc[1].T * scale).astype(bf)
                x_out(s, 0).start()
            else:
                xsend[s, 0] = (kacc[1] * scale).astype(bf)
                x_out(s, 0).start()
                xsend[s, 1] = vacc[1].astype(bf)
                x_out(s, 1).start()
                fin[s, 1] = kacc[0] * scale
                fin[s, 2] = vacc[0]
        each(s, action)

    outs = (q_out, k_out, v_out)

    def finish(s):
        def action(s, kind):
            z_places, x_places = ((1, 2), (0,)) if kind == "queries" else ((0,), (1, 2))
            for a, place in enumerate(z_places):
                for d in (0, 2):
                    @pl.when(live(d))
                    def _():
                        z_back(s, a, d).wait_recv()
                        fin[s, place] += zgot[s, a, d // 2].astype(f32)
                outs[place][s] = fin[s, place].astype(bf)
            for a, place in enumerate(x_places):
                x_out(s, a).wait_recv()
                outs[place][s] = (fin[s, place] + xgot[s, a].astype(f32)).astype(bf)
        each(s, action)

    def drain(s):
        def action(s, kind):
            for a in range(2):
                x_in(s, a, kind).wait_send()
                for d in (0, 2):
                    @pl.when(live(d))
                    def _():
                        z_in(s, a, d, kind).wait_send()
            if kind == "queries":
                for j in range(2):
                    x_stat(s, j).wait_send()
            else:
                for_z_stats(lambda i, r: z_stat(s, i, r).wait_send())
            z_n, x_n = (2, 1) if kind == "queries" else (1, 2)
            for a in range(z_n):
                for d in (0, 2):
                    @pl.when(live(d))
                    def _():
                        z_out(s, a, d).wait_send()
            for a in range(x_n):
                x_out(s, a).wait_send()
        each(s, action)

    send_in(0, 0)
    send_in(0, 1)
    send_in(1, 0)
    scores(0, 0, 6)
    send_stats(0)
    send_in(1, 1)
    send_in(2, 0)
    send_in(2, 1)
    scores(1, 0, 6)
    send_stats(1)
    take_stats(0)
    grads(0)
    scores(2, 0, 6)
    send_stats(2)
    take_stats(1)
    grads(1)
    finish(0)
    take_stats(2)
    grads(2)
    finish(1)
    finish(2)
    for s in range(slots):
        drain(s)

def settle_kernel(a_in, b_in, c_in, a_out, b_out, c_out, held, sems):
    heads = a_in.shape[0]
    pairs = [(i, h) for h in range(heads) for i in range(3)]
    ins, outs = (a_in, b_in, c_in), (a_out, b_out, c_out)
    loads = [pltpu.make_async_copy(ins[i].at[h], held.at[i, h], sems.at[0, i, h]) for i, h in pairs]
    stores = [pltpu.make_async_copy(held.at[i, h], outs[i].at[h], sems.at[1, i, h]) for i, h in pairs]
    for load in loads:
        load.start()
    for load, store in zip(loads, stores):
        load.wait()
        store.start()
    for store in stores:
        store.wait()


def banded(query_in, key_in, value_in, out_grad):
    head_count, frames, rows, cols, depth = query_in.shape
    assert cols == 2 * TILE_C
    tokens = frames * rows * cols
    flat = (head_count, tokens, depth)
    slots = head_count
    bf, f32 = jnp.bfloat16, jnp.float32
    dma = pltpu.SemaphoreType.DMA
    outs = pl.pallas_call(
        banded_kernel,
        out_shape=[jax.ShapeDtypeStruct(flat, bf)] * 3,
        in_specs=[pl.BlockSpec(memory_space=pl.ANY)] * 4,
        out_specs=[pl.BlockSpec(memory_space=pltpu.VMEM)] * 3,
        scratch_shapes=[
            pltpu.VMEM((slots, 2, 3, tokens, depth), bf),
            pltpu.VMEM((slots, 2, 2, tokens, depth), bf),
            pltpu.VMEM((slots, 3, 2, tokens, tokens), f32),
            pltpu.VMEM((slots, 3, 2, tokens, tokens), f32),
            pltpu.VMEM((slots, 3, 2, 8, tokens), f32),
            pltpu.VMEM((slots, 3, 8, tokens), f32),
            pltpu.VMEM((slots, 3, 3, 8, tokens), f32),
            pltpu.VMEM((slots, 3, 8, tokens), f32),
            pltpu.VMEM((slots, 3, tokens, depth), f32),
            pltpu.VMEM((2, tokens, depth), f32),
            pltpu.VMEM((2, tokens, depth), f32),
            pltpu.VMEM((2, depth, tokens), f32),
            pltpu.VMEM((slots, 2, 2, tokens, depth), bf),
            pltpu.VMEM((slots, 2, tokens, depth), bf),
            pltpu.VMEM((slots, 2, 2, tokens, depth), bf),
            pltpu.VMEM((slots, 2, tokens, depth), bf),
            dma((slots, 2, 2)),
            dma((slots, 2)),
            dma((slots, 2)),
            dma((slots, 2, 3)),
            dma((slots, 2, 3)),
            dma((slots, 3, 3)),
            dma((slots, 3, 3)),
            dma((slots, 2)),
            dma((slots, 2)),
            dma((slots, 2, 2)),
            dma((slots, 2, 2)),
        ],
        compiler_params=pltpu.CompilerParams(
            collective_id=0, has_side_effects=True, vmem_limit_bytes=60 * 1024 * 1024
        ),
    )(*(a.reshape(flat) for a in (query_in, key_in, value_in, out_grad)))
    outs = pl.pallas_call(
        settle_kernel,
        out_shape=[jax.ShapeDtypeStruct(flat, bf)] * 3,
        in_specs=[pl.BlockSpec(memory_space=pl.ANY)] * 3,
        out_specs=[pl.BlockSpec(memory_space=pl.ANY)] * 3,
        scratch_shapes=[pltpu.VMEM((3, *flat), bf), dma((2, 3, head_count))],
    )(*outs)
    return tuple(o.reshape(query_in.shape) for o in outs)


def solution(mesh):
    return jax.shard_map(
        banded if mesh.shape["tm"] == 2 else local,
        mesh=mesh,
        in_specs=(
            P("head", "tm", "height", None, None),
            P("head", "tm", "height", None, None),
            P("head", "tm", "height", None, None),
            P("head", "tm", "height", None, None),
        ),
        out_specs=(
            P("head", "tm", "height", None, None),
            P("head", "tm", "height", None, None),
            P("head", "tm", "height", None, None),
        ),
        check_vma=False,
    )
```

```python
import jax
import jax.numpy as jnp
from jax import lax
from jax.experimental import pallas as pl
from jax.experimental.pallas import tpu as pltpu
from jax.sharding import PartitionSpec as P

TILE_C = 8


def shifted(block, axis, distance):
    devices = range(lax.axis_size(axis))
    route = [(i - distance, i) for i in devices if i - distance in devices]
    return lax.ppermute(block, axis, route)


def shortened(x):
    return jax.tree.map(lambda a: a.astype(jnp.bfloat16) if a.dtype == jnp.float32 else a, x)


def extended(x, sides, width):
    for axis, dim in sides:
        size, length = (lax.axis_size(axis), x.shape[dim])
        up = [(i, (i + 1) % size) for i in range(size - 1)]
        down = [(j, i) for i, j in up]
        last = lax.slice_in_dim(x, length - width, length, axis=dim)
        first = lax.slice_in_dim(x, 0, width, axis=dim)
        before = lax.ppermute(last, axis, up)
        after = lax.ppermute(first, axis, down)
        x = jnp.concatenate([before, x, after], axis=dim)
    return x


def neighbour_live():
    offsets = jnp.arange(3, dtype=jnp.int32) - 1
    frame_pos = lax.axis_index("tm") + offsets
    row_pos = lax.axis_index("height") + offsets
    frame_ok = (frame_pos >= 0) & (frame_pos < lax.axis_size("tm"))
    row_ok = (row_pos >= 0) & (row_pos < lax.axis_size("height"))
    return frame_ok[:, None] & row_ok[None, :]


def span_live(neighbour_ok, tile_index, span_start, frame_count, row_count, span_width, col_tile):
    columns = span_start + jnp.arange(span_width, dtype=jnp.int32)
    near_cols = jnp.abs(columns // col_tile - tile_index) <= 1
    live_mask = neighbour_ok[:, :, None, None, None] & near_cols[None, None, None, None, :]
    return jnp.broadcast_to(live_mask, (3, 3, frame_count, row_count, span_width)).reshape(-1)


def scores_of(left_rows, right_rows, live_mask, score_scale):
    raw_scores = (
        jnp.einsum("hqd,hkd->hqk", left_rows, right_rows, preferred_element_type=jnp.float32)
        * score_scale
    )
    return jnp.where(live_mask, raw_scores, -jnp.inf)


def whole_span(array, span_start, span_size, axis_pos):
    return isinstance(span_start, int) and span_start == 0 and (span_size == array.shape[axis_pos])


def cut_span(array, span_start, span_size, axis_pos):
    if whole_span(array, span_start, span_size, axis_pos):
        return array
    return lax.dynamic_slice_in_dim(array, jnp.asarray(span_start, jnp.int32), span_size, axis_pos)


def add_span(array, piece):
    return array + piece


def run_tiles(tile_step, tile_count, col_tile, carried):
    edge_width = 2 * col_tile
    carried = tile_step(0, 0, edge_width, carried)
    return tile_step(tile_count - 1, (tile_count - 2) * col_tile, edge_width, carried)


def send_rows(parts, offset):
    return (
        shifted(parts[0].astype(jnp.bfloat16), "height", offset).astype(jnp.float32),
        shifted(parts[1].astype(jnp.bfloat16), "height", offset).astype(jnp.float32),
    )


def send_frames(parts, offset):
    return shifted((shortened(parts[0]), shortened(parts[1])), "tm", offset)


def local(query_in, key_in, value_in, out_grad):
    head_count, frame_count, row_count, col_count, head_depth = query_in.shape
    col_tile = TILE_C
    tile_count = col_count // col_tile
    score_scale = head_depth ** (-0.5)
    spread_shape = (head_count, 1, 1, frame_count, row_count, col_count, head_depth)
    ext_shape = (head_count, 3, 3, frame_count, row_count, col_count, head_depth)
    stat_shape = (head_count, frame_count, row_count, col_tile)
    neighbour_ok = neighbour_live()
    keys_ext, values_ext = (
        extended(key_in.reshape(spread_shape), (("tm", 1), ("height", 2)), 1),
        extended(value_in.reshape(spread_shape), (("tm", 1), ("height", 2)), 1),
    )

    def query_step(tile_index, span_start, span_width, carried):
        grad_q, row_totals, row_deltas, grad_k, grad_v = carried
        own_start = jnp.asarray(tile_index * col_tile, jnp.int32)
        q_rows = cut_span(query_in, own_start, col_tile, 3).reshape(head_count, -1, head_depth)
        g_rows = cut_span(out_grad, own_start, col_tile, 3).reshape(head_count, -1, head_depth)
        k_span = cut_span(keys_ext, span_start, span_width, 5).reshape(head_count, -1, head_depth)
        v_span = cut_span(values_ext, span_start, span_width, 5).reshape(head_count, -1, head_depth)
        live_mask = span_live(
            neighbour_ok, tile_index, span_start, frame_count, row_count, span_width, col_tile
        )
        scores = scores_of(q_rows, k_span, live_mask[None, None, :], score_scale)
        row_max = jnp.max(scores, axis=-1, keepdims=True)
        log_total = row_max + jnp.log(jnp.sum(jnp.exp(scores - row_max), axis=-1, keepdims=True))
        weights = jnp.exp(scores - log_total)
        weight_bf = weights.astype(jnp.bfloat16)
        attended = jnp.einsum("hqk,hkd->hqd", weight_bf, v_span, preferred_element_type=jnp.float32)
        row_delta = jnp.sum(g_rows.astype(jnp.float32) * attended, axis=-1, keepdims=True)
        d_weights = jnp.einsum("hqd,hkd->hqk", g_rows, v_span, preferred_element_type=jnp.float32)
        d_scores = (weights * (d_weights - row_delta)).astype(jnp.bfloat16)
        grad_piece = (
            jnp.einsum("hqk,hkd->hqd", d_scores, k_span, preferred_element_type=jnp.float32)
            * score_scale
        )
        grad_q = lax.dynamic_update_slice_in_dim(
            grad_q, grad_piece.reshape(stat_shape + (head_depth,)), own_start, 3
        )
        row_totals = lax.dynamic_update_slice_in_dim(
            row_totals, log_total.reshape(stat_shape), own_start, 3
        )
        row_deltas = lax.dynamic_update_slice_in_dim(
            row_deltas, row_delta.reshape(stat_shape), own_start, 3
        )
        span_shape = (head_count, 3, 3, frame_count, row_count, span_width, head_depth)
        key_piece = (
            jnp.einsum("hqk,hqd->hkd", d_scores, q_rows, preferred_element_type=jnp.float32)
            * score_scale
        )
        value_piece = jnp.einsum(
            "hqk,hqd->hkd", weight_bf, g_rows, preferred_element_type=jnp.float32
        )
        grad_k = add_span(grad_k, key_piece.reshape(span_shape))
        grad_v = add_span(grad_v, value_piece.reshape(span_shape))
        return (grad_q, row_totals, row_deltas, grad_k, grad_v)

    stat_full = (head_count, frame_count, row_count, col_count)
    initial = (
        jnp.zeros(query_in.shape, jnp.float32),
        jnp.zeros(stat_full, jnp.float32),
        jnp.zeros(stat_full, jnp.float32),
        jnp.zeros(ext_shape, jnp.float32),
        jnp.zeros(ext_shape, jnp.float32),
    )
    grad_q, row_totals, row_deltas, grad_k, grad_v = run_tiles(
        query_step, tile_count, col_tile, initial
    )
    query_grad = grad_q.astype(jnp.bfloat16)
    from_above = send_rows((grad_k[:, :, 0], grad_v[:, :, 0]), -1)
    from_below = send_rows((grad_k[:, :, 2], grad_v[:, :, 2]), 1)
    part_k = grad_k[:, :, 1] + from_above[0] + from_below[0]
    part_v = grad_v[:, :, 1] + from_above[1] + from_below[1]
    from_next = send_frames((part_k[:, 0], part_v[:, 0]), -1)
    from_prev = send_frames((part_k[:, 2], part_v[:, 2]), 1)
    key_total = part_k[:, 1] + from_next[0] + from_prev[0]
    value_total = part_v[:, 1] + from_next[1] + from_prev[1]
    return (query_grad, key_total.astype(jnp.bfloat16), value_total.astype(jnp.bfloat16))


LOG2_E = 1.4426950408889634


def job_kinds(slot, slots):
    return ("keys" if slot < slots // 2 else "queries", "keys" if slot < slots - slots // 2 else "queries")


def banded_kernel(
    q_in, k_in, v_in, g_in, q_out, k_out, v_out,
    zb, xb, probs, dws, block_stats, sloc, sfar, total, fin, kacc, vacc, qacc,
    zsend, xsend, zgot, xgot,
    loc, xis, xir, zis, zir, ss, sr, xos, xor_, zos, zor,
):
    slots, tokens, depth = q_in.shape
    scale = depth ** (-0.5)
    rate = scale * LOG2_E
    f32, bf = jnp.float32, jnp.bfloat16
    x = lax.axis_index("tm")
    z = lax.axis_index("height")
    z_count = lax.axis_size("height")
    parity = lax.rem(lax.axis_index("head"), 2)
    other = 1 - x

    def at_z(distance):
        return (z + distance >= 0) & (z + distance < z_count)

    def live(i):
        return at_z(i - 1)

    def each(s, action):
        kinds = job_kinds(s, slots)
        if kinds[0] == kinds[1]:
            action(s, kinds[0])
        else:
            for p in range(2):
                @pl.when(parity == p)
                def _():
                    action(s, kinds[p])

    def x_side(kind):
        return (q_in, g_in) if kind == "queries" else (k_in, v_in)

    def z_side(kind):
        return (k_in, v_in) if kind == "queries" else (q_in, g_in)

    def key_first(kind, i, j):
        return (zb, i, xb, j) if kind == "queries" else (xb, j, zb, i)

    groups = tokens // 128
    nothing = jnp.concatenate(
        [jnp.full((groups, 128), -jnp.inf, f32), jnp.zeros((groups, 128), f32)], axis=0
    )
    block_stats[:, :, :, 0:1, :] = jnp.full((slots, 3, 2, 1, tokens), -jnp.inf, f32)
    block_stats[:, :, :, 1:8, :] = jnp.zeros((slots, 3, 2, 7, tokens), f32)
    sfar[...] = jnp.broadcast_to(nothing, sfar.shape)

    def own_copies(s, a, kind):
        return [
            pltpu.make_async_copy(x_side(kind)[a].at[s], xb.at[s, a, 0], loc.at[s, a, 0]),
            pltpu.make_async_copy(z_side(kind)[a].at[s], zb.at[s, a, 1], loc.at[s, a, 1]),
        ]

    def start_own(s, kind):
        for a in range(2):
            for copy in own_copies(s, a, kind):
                copy.start()

    barrier = pltpu.get_barrier_semaphore()
    pl.semaphore_signal(barrier, inc=1, device_id={"tm": other})
    for distance in (-2, -1, 1, 2):
        @pl.when(at_z(distance))
        def _():
            pl.semaphore_signal(barrier, inc=1, device_id={"height": z + distance})
    for s in range(slots):
        each(s, start_own)
    pl.semaphore_wait(barrier, 1 + sum(jnp.where(at_z(n), 1, 0) for n in (-2, -1, 1, 2)))

    def x_in(s, a, kind):
        return pltpu.make_async_remote_copy(
            src_ref=x_side(kind)[a].at[s], dst_ref=xb.at[s, a, 1],
            send_sem=xis.at[s, a], recv_sem=xir.at[s, a], device_id={"tm": other},
        )

    def z_in(s, a, d, kind):
        return pltpu.make_async_remote_copy(
            src_ref=z_side(kind)[a].at[s], dst_ref=zb.at[s, a, 2 - d],
            send_sem=zis.at[s, a, d], recv_sem=zir.at[s, a, 2 - d], device_id={"height": z + d - 1},
        )

    def z_arrived(s, a, i, kind):
        return pltpu.make_async_remote_copy(
            src_ref=z_side(kind)[a].at[s], dst_ref=zb.at[s, a, i],
            send_sem=zis.at[s, a, 0], recv_sem=zir.at[s, a, i], device_id={"height": z + i - 1},
        )

    def send_in(s, a):
        def action(s, kind):
            x_in(s, a, kind).start()
            for d in (0, 2):
                @pl.when(live(d))
                def _():
                    z_in(s, a, d, kind).start()
        each(s, action)

    def folded(block):
        return block.reshape(tokens // 8, 8, tokens)

    def row(ref, n):
        return ref[n:n + 1, :]

    def arrive(s, a, i, j, kind, turn):
        @pl.when(turn == 1)
        def _():
            x_in(s, a, kind).wait_recv()

        @pl.when((turn > 1) & (j == 0))
        def _():
            z_arrived(s, a, i, kind).wait_recv()

    def product(s, a, i, j, kind):
        kz, ki, qz, qi = key_first(kind, i, j)
        return lax.dot_general(
            kz[s, a, ki], qz[s, a, qi], (((1,), (1,)), ((), ())), preferred_element_type=f32
        )

    def score_block(s, i, j, kind):
        raw = product(s, 0, i, j, kind)
        top = jnp.max(jnp.max(folded(raw), axis=0), axis=0, keepdims=True)
        prob = jnp.exp2((raw - top) * rate)
        probs[s, i, j] = prob
        out = block_stats.at[s, i, j]
        out[0:1, :] = top * rate
        out[1:2, :] = jnp.sum(jnp.sum(folded(prob), axis=0), axis=0, keepdims=True)

    def slope_block(s, i, j, kind):
        dw = product(s, 1, i, j, kind)
        dws[s, i, j] = dw
        pull = probs[s, i, j] * dw
        out = block_stats.at[s, i, j]
        out[2:3, :] = jnp.sum(jnp.sum(folded(pull), axis=0), axis=0, keepdims=True)

    def sweep(s, a, first, last):
        body = (score_block, slope_block)[a]

        def action(s, kind):
            if first == 0:
                for copy in own_copies(s, a, kind):
                    copy.wait()

            @pl.loop(first, last)
            def _(turn):
                i = lax.rem(1 + 2 * (turn // 2), 3)
                j = lax.rem(turn, 2)

                @pl.when(live(i))
                def _():
                    arrive(s, a, i, j, kind, turn)
                    body(s, i, j, kind)
        each(s, action)

    def own_part(s):
        sweep(s, 0, 0, 1)
        sweep(s, 1, 0, 1)

    def weighed(tops, pairs):
        top = tops[0]
        for t in tops[1:]:
            top = jnp.maximum(top, t)
        factors = [jnp.exp2(t - top) for t in tops]
        mass = sum(f * m for f, (m, _) in zip(factors, pairs))
        pull = sum(f * d for f, (_, d) in zip(factors, pairs))
        return top + jnp.log(mass) * LOG2_E, pull / mass

    def merge_blocks(s, b, parts):
        tops = [row(p, 0) for p in parts]
        pairs = [(row(p, 1), row(p, 2)) for p in parts]
        for n, value in enumerate(weighed(tops, pairs)):
            for g in range(groups):
                r = n * groups + g
                sloc[s, b, r:r + 1, :] = value[:, g * 128:(g + 1) * 128]

    def merge_devices(s, b, far):
        parts = [ref[...] for ref in [sloc.at[s, b]] + far]
        level, delta = weighed(
            [p[:groups] for p in parts], [(1.0, p[groups:]) for p in parts]
        )
        for n, value in enumerate((level, delta)):
            for g in range(groups):
                total[s, b, n:n + 1, g * 128:(g + 1) * 128] = value[g:g + 1, :]

    def x_stat(s, j):
        return pltpu.make_async_remote_copy(
            src_ref=sloc.at[s, j], dst_ref=sfar.at[s, 1 - j, 0],
            send_sem=ss.at[s, j, 0], recv_sem=sr.at[s, 1 - j, 0], device_id={"tm": other},
        )

    def z_stat(s, i, r):
        return pltpu.make_async_remote_copy(
            src_ref=sloc.at[s, i], dst_ref=sfar.at[s, 2 - r, 2 - i],
            send_sem=ss.at[s, i, r], recv_sem=sr.at[s, 2 - r, 2 - i],
            device_id={"height": z + i + r - 2},
        )

    def z_stat_arrived(s, i, r):
        return pltpu.make_async_remote_copy(
            src_ref=sloc.at[s, i], dst_ref=sfar.at[s, i, r],
            send_sem=ss.at[s, i, r], recv_sem=sr.at[s, i, r],
            device_id={"height": z + i + r - 2},
        )

    def for_z_stats(action):
        for i in range(3):
            for r in range(3):
                if r != 2 - i:
                    @pl.when(live(i) & at_z(i + r - 2))
                    def _():
                        action(i, r)

    def send_stats(s):
        def action(s, kind):
            if kind == "queries":
                for j in (1, 0):
                    merge_blocks(s, j, [block_stats.at[s, i, j] for i in range(3)])
                    x_stat(s, j).start()
            else:
                for i in range(3):
                    @pl.when(live(i))
                    def _():
                        merge_blocks(s, i, [block_stats.at[s, i, j] for j in range(2)])
                for_z_stats(lambda i, r: z_stat(s, i, r).start())
        each(s, action)

    def take_stats(s):
        def action(s, kind):
            if kind == "queries":
                for j in range(2):
                    x_stat(s, 1 - j).wait_recv()
                    merge_devices(s, j, [sfar.at[s, j, 0]])
            else:
                for_z_stats(lambda i, r: z_stat_arrived(s, i, r).wait_recv())
                for i in range(3):
                    @pl.when(live(i))
                    def _():
                        merge_devices(s, i, [sfar.at[s, i, r] for r in range(3) if r != 2 - i])
        each(s, action)

    def z_out(s, a, d):
        return pltpu.make_async_remote_copy(
            src_ref=zsend.at[s, a, d // 2], dst_ref=zgot.at[s, a, 1 - d // 2],
            send_sem=zos.at[s, a, d // 2], recv_sem=zor.at[s, a, 1 - d // 2],
            device_id={"height": z + d - 1},
        )

    def z_back(s, a, d):
        return pltpu.make_async_remote_copy(
            src_ref=zsend.at[s, a, d // 2], dst_ref=zgot.at[s, a, d // 2],
            send_sem=zos.at[s, a, d // 2], recv_sem=zor.at[s, a, d // 2],
            device_id={"height": z + d - 1},
        )

    def x_out(s, a):
        return pltpu.make_async_remote_copy(
            src_ref=xsend.at[s, a], dst_ref=xgot.at[s, a],
            send_sem=xos.at[s, a], recv_sem=xor_.at[s, a], device_id={"tm": other},
        )

    def grad_block(s, i, kind):
        pieces = []
        for j in range(2):
            kz, ki, qz, qi = key_first(kind, i, j)
            goal = total.at[s, j if kind == "queries" else i]
            weight = probs[s, i, j] * jnp.exp2(row(block_stats.at[s, i, j], 0) - row(goal, 0))
            ds = (weight * (dws[s, i, j] - row(goal, 1))).astype(bf)
            dv = jnp.dot(weight.astype(bf), qz[s, 1, qi], preferred_element_type=f32)
            dk = jnp.dot(ds, qz[s, 0, qi], preferred_element_type=f32)
            dq = lax.dot_general(
                kz[s, 0, ki], ds, (((0,), (0,)), ((), ())), preferred_element_type=f32
            )
            pieces.append((dk, dv, dq))
        if kind == "queries":
            for j in range(2):
                qacc[j] += pieces[j][2]
            done = ((pieces[0][0] + pieces[1][0]) * scale, pieces[0][1] + pieces[1][1])
            places = (1, 2)
        else:
            for j in range(2):
                kacc[j] += pieces[j][0]
                vacc[j] += pieces[j][1]
            done = ((pieces[0][2] + pieces[1][2]).T * scale,)
            places = (0,)

        @pl.when(i == 1)
        def _():
            for value, place in zip(done, places):
                fin[s, place] = value

        @pl.when(i != 1)
        def _():
            for a, value in enumerate(done):
                zsend[s, a, i // 2] = value.astype(bf)
                z_out(s, a, i).start()

    def grads(s, first, last, centre_first=False):
        def action(s, kind):
            if first == 0:
                if kind == "queries":
                    qacc[...] = jnp.zeros_like(qacc)
                else:
                    kacc[...] = jnp.zeros_like(kacc)
                    vacc[...] = jnp.zeros_like(vacc)

            @pl.loop(first, last)
            def _(turn):
                i = lax.rem((1 if centre_first else 0) + 2 * turn, 3)

                @pl.when(live(i))
                def _():
                    grad_block(s, i, kind)

            if last < 3:
                return
            if kind == "queries":
                xsend[s, 0] = (qacc[1].T * scale).astype(bf)
                x_out(s, 0).start()
                fin[s, 0] = qacc[0].T * scale
            else:
                xsend[s, 0] = (kacc[1] * scale).astype(bf)
                x_out(s, 0).start()
                xsend[s, 1] = vacc[1].astype(bf)
                if s > 0:
                    x_out(s, 1).start()
                fin[s, 1] = kacc[0] * scale
                fin[s, 2] = vacc[0]
        each(s, action)

    def late_x_out(s):
        def action(s, kind):
            if kind == "keys":
                x_out(s, 1).start()
        each(s, action)

    outs = (q_out, k_out, v_out)

    def finish(s):
        def action(s, kind):
            z_places, x_places = ((1, 2), (0,)) if kind == "queries" else ((0,), (1, 2))
            for a, place in enumerate(z_places):
                for d in (0, 2):
                    @pl.when(live(d))
                    def _():
                        z_back(s, a, d).wait_recv()
                        fin[s, place] += zgot[s, a, d // 2].astype(f32)
                outs[place][s] = fin[s, place].astype(bf)
            for a, place in enumerate(x_places):
                x_out(s, a).wait_recv()
                outs[place][s] = (fin[s, place] + xgot[s, a].astype(f32)).astype(bf)
        each(s, action)

    def drain(s):
        def action(s, kind):
            for a in range(2):
                x_in(s, a, kind).wait_send()
                for d in (0, 2):
                    @pl.when(live(d))
                    def _():
                        z_in(s, a, d, kind).wait_send()
            if kind == "queries":
                for j in range(2):
                    x_stat(s, j).wait_send()
            else:
                for_z_stats(lambda i, r: z_stat(s, i, r).wait_send())
            z_n, x_n = (2, 1) if kind == "queries" else (1, 2)
            for a in range(z_n):
                for d in (0, 2):
                    @pl.when(live(d))
                    def _():
                        z_out(s, a, d).wait_send()
            for a in range(x_n):
                x_out(s, a).wait_send()
        each(s, action)

    send_in(0, 0)
    send_in(0, 1)
    send_in(1, 0)
    for s in range(slots):
        own_part(s)
    sweep(0, 0, 1, 6)
    sweep(0, 1, 1, 6)
    send_stats(0)
    send_in(1, 1)
    send_in(2, 0)
    sweep(1, 0, 1, 6)
    take_stats(0)
    grads(0, 0, 1, True)
    sweep(1, 1, 1, 6)
    send_stats(1)
    send_in(2, 1)
    grads(0, 1, 3, True)
    sweep(2, 0, 1, 6)
    take_stats(1)
    grads(1, 0, 1)
    sweep(2, 1, 1, 6)
    send_stats(2)
    late_x_out(0)
    grads(1, 1, 3)
    take_stats(2)
    grads(2, 0, 3)
    for s in range(slots):
        finish(s)
    for s in range(slots):
        drain(s)


def settle_kernel(a_in, b_in, c_in, a_out, b_out, c_out, sems):
    pairs = ((a_in, a_out), (b_in, b_out), (c_in, c_out))
    copies = [pltpu.make_async_copy(src, dst, sems.at[i]) for i, (src, dst) in enumerate(pairs)]
    for copy in copies:
        copy.start()
    for copy in copies:
        copy.wait()


def banded(query_in, key_in, value_in, out_grad):
    head_count, frames, rows, cols, depth = query_in.shape
    assert cols == 2 * TILE_C
    tokens = frames * rows * cols
    flat = (head_count, tokens, depth)
    slots = head_count
    bf, f32 = jnp.bfloat16, jnp.float32
    dma = pltpu.SemaphoreType.DMA
    outs = pl.pallas_call(
        banded_kernel,
        out_shape=[pltpu.VMEM(flat, bf)] * 3,
        in_specs=[pl.BlockSpec(memory_space=pl.ANY)] * 4,
        out_specs=[pl.BlockSpec(memory_space=pltpu.VMEM)] * 3,
        scratch_shapes=[
            pltpu.VMEM((slots, 2, 3, tokens, depth), bf),
            pltpu.VMEM((slots, 2, 2, tokens, depth), bf),
            pltpu.VMEM((slots, 3, 2, tokens, tokens), f32),
            pltpu.VMEM((slots, 3, 2, tokens, tokens), f32),
            pltpu.VMEM((slots, 3, 2, 8, tokens), f32),
            pltpu.VMEM((slots, 3, tokens // 64, 128), f32),
            pltpu.VMEM((slots, 3, 3, tokens // 64, 128), f32),
            pltpu.VMEM((slots, 3, 8, tokens), f32),
            pltpu.VMEM((slots, 3, tokens, depth), f32),
            pltpu.VMEM((2, tokens, depth), f32),
            pltpu.VMEM((2, tokens, depth), f32),
            pltpu.VMEM((2, depth, tokens), f32),
            pltpu.VMEM((slots, 2, 2, tokens, depth), bf),
            pltpu.VMEM((slots, 2, tokens, depth), bf),
            pltpu.VMEM((slots, 2, 2, tokens, depth), bf),
            pltpu.VMEM((slots, 2, tokens, depth), bf),
            dma((slots, 2, 2)),
            dma((slots, 2)),
            dma((slots, 2)),
            dma((slots, 2, 3)),
            dma((slots, 2, 3)),
            dma((slots, 3, 3)),
            dma((slots, 3, 3)),
            dma((slots, 2)),
            dma((slots, 2)),
            dma((slots, 2, 2)),
            dma((slots, 2, 2)),
        ],
        compiler_params=pltpu.CompilerParams(
            collective_id=0, has_side_effects=True, vmem_limit_bytes=60 * 1024 * 1024
        ),
    )(*(a.reshape(flat) for a in (query_in, key_in, value_in, out_grad)))
    outs = pl.pallas_call(
        settle_kernel,
        out_shape=[jax.ShapeDtypeStruct(flat, bf)] * 3,
        in_specs=[pl.BlockSpec(memory_space=pl.ANY)] * 3,
        out_specs=[pl.BlockSpec(memory_space=pl.ANY)] * 3,
        scratch_shapes=[dma((3,))],
    )(*(pltpu.with_memory_space_constraint(o, pltpu.VMEM) for o in outs))
    return tuple(o.reshape(query_in.shape) for o in outs)


def solution(mesh):
    return jax.shard_map(
        banded if mesh.shape["tm"] == 2 else local,
        mesh=mesh,
        in_specs=(
            P("head", "tm", "height", None, None),
            P("head", "tm", "height", None, None),
            P("head", "tm", "height", None, None),
            P("head", "tm", "height", None, None),
        ),
        out_specs=(
            P("head", "tm", "height", None, None),
            P("head", "tm", "height", None, None),
            P("head", "tm", "height", None, None),
        ),
        check_vma=False,
    )
```

```python
import jax
import jax.numpy as jnp
from jax import lax
from jax.experimental import pallas as pl
from jax.experimental.pallas import tpu as pltpu
from jax.sharding import PartitionSpec as P

TILE_C = 8


def shifted(block, axis, distance):
    devices = range(lax.axis_size(axis))
    route = [(i - distance, i) for i in devices if i - distance in devices]
    return lax.ppermute(block, axis, route)


def shortened(x):
    return jax.tree.map(lambda a: a.astype(jnp.bfloat16) if a.dtype == jnp.float32 else a, x)


def extended(x, sides, width):
    for axis, dim in sides:
        size, length = (lax.axis_size(axis), x.shape[dim])
        up = [(i, (i + 1) % size) for i in range(size - 1)]
        down = [(j, i) for i, j in up]
        last = lax.slice_in_dim(x, length - width, length, axis=dim)
        first = lax.slice_in_dim(x, 0, width, axis=dim)
        before = lax.ppermute(last, axis, up)
        after = lax.ppermute(first, axis, down)
        x = jnp.concatenate([before, x, after], axis=dim)
    return x


def neighbour_live():
    offsets = jnp.arange(3, dtype=jnp.int32) - 1
    frame_pos = lax.axis_index("tm") + offsets
    row_pos = lax.axis_index("height") + offsets
    frame_ok = (frame_pos >= 0) & (frame_pos < lax.axis_size("tm"))
    row_ok = (row_pos >= 0) & (row_pos < lax.axis_size("height"))
    return frame_ok[:, None] & row_ok[None, :]


def span_live(neighbour_ok, tile_index, span_start, frame_count, row_count, span_width, col_tile):
    columns = span_start + jnp.arange(span_width, dtype=jnp.int32)
    near_cols = jnp.abs(columns // col_tile - tile_index) <= 1
    live_mask = neighbour_ok[:, :, None, None, None] & near_cols[None, None, None, None, :]
    return jnp.broadcast_to(live_mask, (3, 3, frame_count, row_count, span_width)).reshape(-1)


def scores_of(left_rows, right_rows, live_mask, score_scale):
    raw_scores = (
        jnp.einsum("hqd,hkd->hqk", left_rows, right_rows, preferred_element_type=jnp.float32)
        * score_scale
    )
    return jnp.where(live_mask, raw_scores, -jnp.inf)


def whole_span(array, span_start, span_size, axis_pos):
    return isinstance(span_start, int) and span_start == 0 and (span_size == array.shape[axis_pos])


def cut_span(array, span_start, span_size, axis_pos):
    if whole_span(array, span_start, span_size, axis_pos):
        return array
    return lax.dynamic_slice_in_dim(array, jnp.asarray(span_start, jnp.int32), span_size, axis_pos)


def add_span(array, piece):
    return array + piece


def run_tiles(tile_step, tile_count, col_tile, carried):
    edge_width = 2 * col_tile
    carried = tile_step(0, 0, edge_width, carried)
    return tile_step(tile_count - 1, (tile_count - 2) * col_tile, edge_width, carried)


def send_rows(parts, offset):
    return (
        shifted(parts[0].astype(jnp.bfloat16), "height", offset).astype(jnp.float32),
        shifted(parts[1].astype(jnp.bfloat16), "height", offset).astype(jnp.float32),
    )


def send_frames(parts, offset):
    return shifted((shortened(parts[0]), shortened(parts[1])), "tm", offset)


def local(query_in, key_in, value_in, out_grad):
    head_count, frame_count, row_count, col_count, head_depth = query_in.shape
    col_tile = TILE_C
    tile_count = col_count // col_tile
    score_scale = head_depth ** (-0.5)
    spread_shape = (head_count, 1, 1, frame_count, row_count, col_count, head_depth)
    ext_shape = (head_count, 3, 3, frame_count, row_count, col_count, head_depth)
    stat_shape = (head_count, frame_count, row_count, col_tile)
    neighbour_ok = neighbour_live()
    keys_ext, values_ext = (
        extended(key_in.reshape(spread_shape), (("tm", 1), ("height", 2)), 1),
        extended(value_in.reshape(spread_shape), (("tm", 1), ("height", 2)), 1),
    )

    def query_step(tile_index, span_start, span_width, carried):
        grad_q, row_totals, row_deltas, grad_k, grad_v = carried
        own_start = jnp.asarray(tile_index * col_tile, jnp.int32)
        q_rows = cut_span(query_in, own_start, col_tile, 3).reshape(head_count, -1, head_depth)
        g_rows = cut_span(out_grad, own_start, col_tile, 3).reshape(head_count, -1, head_depth)
        k_span = cut_span(keys_ext, span_start, span_width, 5).reshape(head_count, -1, head_depth)
        v_span = cut_span(values_ext, span_start, span_width, 5).reshape(head_count, -1, head_depth)
        live_mask = span_live(
            neighbour_ok, tile_index, span_start, frame_count, row_count, span_width, col_tile
        )
        scores = scores_of(q_rows, k_span, live_mask[None, None, :], score_scale)
        row_max = jnp.max(scores, axis=-1, keepdims=True)
        log_total = row_max + jnp.log(jnp.sum(jnp.exp(scores - row_max), axis=-1, keepdims=True))
        weights = jnp.exp(scores - log_total)
        weight_bf = weights.astype(jnp.bfloat16)
        attended = jnp.einsum("hqk,hkd->hqd", weight_bf, v_span, preferred_element_type=jnp.float32)
        row_delta = jnp.sum(g_rows.astype(jnp.float32) * attended, axis=-1, keepdims=True)
        d_weights = jnp.einsum("hqd,hkd->hqk", g_rows, v_span, preferred_element_type=jnp.float32)
        d_scores = (weights * (d_weights - row_delta)).astype(jnp.bfloat16)
        grad_piece = (
            jnp.einsum("hqk,hkd->hqd", d_scores, k_span, preferred_element_type=jnp.float32)
            * score_scale
        )
        grad_q = lax.dynamic_update_slice_in_dim(
            grad_q, grad_piece.reshape(stat_shape + (head_depth,)), own_start, 3
        )
        row_totals = lax.dynamic_update_slice_in_dim(
            row_totals, log_total.reshape(stat_shape), own_start, 3
        )
        row_deltas = lax.dynamic_update_slice_in_dim(
            row_deltas, row_delta.reshape(stat_shape), own_start, 3
        )
        span_shape = (head_count, 3, 3, frame_count, row_count, span_width, head_depth)
        key_piece = (
            jnp.einsum("hqk,hqd->hkd", d_scores, q_rows, preferred_element_type=jnp.float32)
            * score_scale
        )
        value_piece = jnp.einsum(
            "hqk,hqd->hkd", weight_bf, g_rows, preferred_element_type=jnp.float32
        )
        grad_k = add_span(grad_k, key_piece.reshape(span_shape))
        grad_v = add_span(grad_v, value_piece.reshape(span_shape))
        return (grad_q, row_totals, row_deltas, grad_k, grad_v)

    stat_full = (head_count, frame_count, row_count, col_count)
    initial = (
        jnp.zeros(query_in.shape, jnp.float32),
        jnp.zeros(stat_full, jnp.float32),
        jnp.zeros(stat_full, jnp.float32),
        jnp.zeros(ext_shape, jnp.float32),
        jnp.zeros(ext_shape, jnp.float32),
    )
    grad_q, row_totals, row_deltas, grad_k, grad_v = run_tiles(
        query_step, tile_count, col_tile, initial
    )
    query_grad = grad_q.astype(jnp.bfloat16)
    from_above = send_rows((grad_k[:, :, 0], grad_v[:, :, 0]), -1)
    from_below = send_rows((grad_k[:, :, 2], grad_v[:, :, 2]), 1)
    part_k = grad_k[:, :, 1] + from_above[0] + from_below[0]
    part_v = grad_v[:, :, 1] + from_above[1] + from_below[1]
    from_next = send_frames((part_k[:, 0], part_v[:, 0]), -1)
    from_prev = send_frames((part_k[:, 2], part_v[:, 2]), 1)
    key_total = part_k[:, 1] + from_next[0] + from_prev[0]
    value_total = part_v[:, 1] + from_next[1] + from_prev[1]
    return (query_grad, key_total.astype(jnp.bfloat16), value_total.astype(jnp.bfloat16))


LOG2_E = 1.4426950408889634


def job_kinds(slot, slots):
    return ("keys" if slot < slots // 2 else "queries", "keys" if slot < slots - slots // 2 else "queries")


def banded_kernel(
    q_in, k_in, v_in, g_in, q_out, k_out, v_out,
    zb, xb, probs, dws, block_stats, sloc, sfar, total, fin, kacc, vacc, qacc,
    zsend, xsend, zgot, xgot,
    loc, xis, xir, zis, zir, ss, sr, xos, xor_, zos, zor,
):
    slots, tokens, depth = q_in.shape
    scale = depth ** (-0.5)
    rate = scale * LOG2_E
    f32, bf = jnp.float32, jnp.bfloat16
    x = lax.axis_index("tm")
    z = lax.axis_index("height")
    z_count = lax.axis_size("height")
    parity = lax.rem(lax.axis_index("head"), 2)
    other = 1 - x

    def at_z(distance):
        return (z + distance >= 0) & (z + distance < z_count)

    def live(i):
        return at_z(i - 1)

    def each(s, action):
        kinds = job_kinds(s, slots)
        if kinds[0] == kinds[1]:
            action(s, kinds[0])
        else:
            for p in range(2):
                @pl.when(parity == p)
                def _():
                    action(s, kinds[p])

    def x_side(kind):
        return (q_in, g_in) if kind == "queries" else (k_in, v_in)

    def z_side(kind):
        return (k_in, v_in) if kind == "queries" else (q_in, g_in)

    def key_first(kind, i, j):
        return (zb, i, xb, j) if kind == "queries" else (xb, j, zb, i)

    groups = tokens // 128
    nothing = jnp.concatenate(
        [jnp.full((groups, 128), -jnp.inf, f32), jnp.zeros((groups, 128), f32)], axis=0
    )
    block_stats[:, :, :, 0:1, :] = jnp.full((slots, 3, 2, 1, tokens), -jnp.inf, f32)
    block_stats[:, :, :, 1:8, :] = jnp.zeros((slots, 3, 2, 7, tokens), f32)
    sfar[...] = jnp.broadcast_to(nothing, sfar.shape)

    def own_copies(s, a, kind):
        return [
            pltpu.make_async_copy(x_side(kind)[a].at[s], xb.at[s, a, 0], loc.at[s, a, 0]),
            pltpu.make_async_copy(z_side(kind)[a].at[s], zb.at[s, a, 1], loc.at[s, a, 1]),
        ]

    def start_own(s, kind):
        for a in range(2):
            for copy in own_copies(s, a, kind):
                copy.start()

    barrier = pltpu.get_barrier_semaphore()
    pl.semaphore_signal(barrier, inc=1, device_id={"tm": other})
    for distance in (-1, 1):
        @pl.when(at_z(distance))
        def _():
            pl.semaphore_signal(barrier, inc=1, device_id={"height": z + distance})
    for s in range(slots):
        each(s, start_own)
    pl.semaphore_wait(barrier, 1 + sum(jnp.where(at_z(n), 1, 0) for n in (-1, 1)))

    def x_in(s, a, kind):
        return pltpu.make_async_remote_copy(
            src_ref=x_side(kind)[a].at[s], dst_ref=xb.at[s, a, 1],
            send_sem=xis.at[s, a], recv_sem=xir.at[s, a], device_id={"tm": other},
        )

    def z_in(s, a, d, kind):
        return pltpu.make_async_remote_copy(
            src_ref=z_side(kind)[a].at[s], dst_ref=zb.at[s, a, 2 - d],
            send_sem=zis.at[s, a, d], recv_sem=zir.at[s, a, 2 - d], device_id={"height": z + d - 1},
        )

    def z_arrived(s, a, i, kind):
        return pltpu.make_async_remote_copy(
            src_ref=z_side(kind)[a].at[s], dst_ref=zb.at[s, a, i],
            send_sem=zis.at[s, a, 0], recv_sem=zir.at[s, a, i], device_id={"height": z + i - 1},
        )

    def send_in(s, a):
        def action(s, kind):
            x_in(s, a, kind).start()
            for d in (0, 2):
                @pl.when(live(d))
                def _():
                    z_in(s, a, d, kind).start()
        each(s, action)

    def folded(block):
        return block.reshape(tokens // 8, 8, tokens)

    def row(ref, n):
        return ref[n:n + 1, :]

    def product(s, a, i, j, kind):
        kz, ki, qz, qi = key_first(kind, i, j)
        return lax.dot_general(
            kz[s, a, ki], qz[s, a, qi], (((1,), (1,)), ((), ())), preferred_element_type=f32
        )

    def column(op, block):
        return op(op(folded(block), axis=0), axis=0, keepdims=True)

    def blocks(s, i, columns, kind, arrays):
        raws = [product(s, 0, i, j, kind) for j in columns] if 0 in arrays else None
        slopes = [product(s, 1, i, j, kind) for j in columns] if 1 in arrays else None
        for n, j in enumerate(columns):
            out = block_stats.at[s, i, j]
            if raws:
                top = column(jnp.max, raws[n])
                prob = jnp.exp2((raws[n] - top) * rate)
                probs[s, i, j] = prob
                out[0:1, :] = top * rate
                out[1:2, :] = column(jnp.sum, prob)
            else:
                prob = probs[s, i, j]
            if slopes:
                dws[s, i, j] = slopes[n]
                out[2:3, :] = column(jnp.sum, prob * slopes[n])

    def own_part(s):
        def action(s, kind):
            for a in range(2):
                for copy in own_copies(s, a, kind):
                    copy.wait()
            blocks(s, 1, (0,), kind, (0, 1))
        each(s, action)

    def far_part(s, arrays):
        def action(s, kind):
            for a in arrays:
                x_in(s, a, kind).wait_recv()
            blocks(s, 1, (1,), kind, arrays)

            @pl.loop(0, 2)
            def _(turn):
                i = 2 * turn

                @pl.when(live(i))
                def _():
                    for a in arrays:
                        z_arrived(s, a, i, kind).wait_recv()
                    blocks(s, i, (0, 1), kind, arrays)
        each(s, action)

    def weighed(tops, pairs):
        top = tops[0]
        for t in tops[1:]:
            top = jnp.maximum(top, t)
        factors = [jnp.exp2(t - top) for t in tops]
        mass = sum(f * m for f, (m, _) in zip(factors, pairs))
        pull = sum(f * d for f, (_, d) in zip(factors, pairs))
        return top + jnp.log(mass) * LOG2_E, pull / mass

    def merge_blocks(s, b, parts):
        tops = [row(p, 0) for p in parts]
        pairs = [(row(p, 1), row(p, 2)) for p in parts]
        for n, value in enumerate(weighed(tops, pairs)):
            for g in range(groups):
                r = n * groups + g
                sloc[s, b, r:r + 1, :] = value[:, g * 128:(g + 1) * 128]

    def merge_devices(s, b, far):
        parts = [ref[...] for ref in [sloc.at[s, b]] + far]
        level, delta = weighed(
            [p[:groups] for p in parts], [(1.0, p[groups:]) for p in parts]
        )
        for n, value in enumerate((level, delta)):
            for g in range(groups):
                total[s, b, n:n + 1, g * 128:(g + 1) * 128] = value[g:g + 1, :]

    def x_stat(s, j):
        return pltpu.make_async_remote_copy(
            src_ref=sloc.at[s, j], dst_ref=sfar.at[s, 1 - j, 0],
            send_sem=ss.at[s, j, 0], recv_sem=sr.at[s, 1 - j, 0], device_id={"tm": other},
        )

    def z_stat(s, i, r):
        return pltpu.make_async_remote_copy(
            src_ref=sloc.at[s, i], dst_ref=sfar.at[s, 2 - r, 2 - i],
            send_sem=ss.at[s, i, r], recv_sem=sr.at[s, 2 - r, 2 - i],
            device_id={"height": z + i + r - 2},
        )

    def z_stat_arrived(s, i, r):
        return pltpu.make_async_remote_copy(
            src_ref=sloc.at[s, i], dst_ref=sfar.at[s, i, r],
            send_sem=ss.at[s, i, r], recv_sem=sr.at[s, i, r],
            device_id={"height": z + i + r - 2},
        )

    def for_z_stats(action):
        for i in range(3):
            for r in range(3):
                if r != 2 - i:
                    @pl.when(live(i) & at_z(i + r - 2))
                    def _():
                        action(i, r)

    def send_stats(s):
        def action(s, kind):
            if kind == "queries":
                for j in (1, 0):
                    merge_blocks(s, j, [block_stats.at[s, i, j] for i in range(3)])
                    x_stat(s, j).start()
            else:
                for i in range(3):
                    @pl.when(live(i))
                    def _():
                        merge_blocks(s, i, [block_stats.at[s, i, j] for j in range(2)])
                for_z_stats(lambda i, r: z_stat(s, i, r).start())
        each(s, action)

    def take_stats(s):
        def action(s, kind):
            if kind == "queries":
                for j in range(2):
                    x_stat(s, 1 - j).wait_recv()
                    merge_devices(s, j, [sfar.at[s, j, 0]])
            else:
                for_z_stats(lambda i, r: z_stat_arrived(s, i, r).wait_recv())
                for i in range(3):
                    @pl.when(live(i))
                    def _():
                        merge_devices(s, i, [sfar.at[s, i, r] for r in range(3) if r != 2 - i])
        each(s, action)

    def z_out(s, a, d):
        return pltpu.make_async_remote_copy(
            src_ref=zsend.at[s, a, d // 2], dst_ref=zgot.at[s, a, 1 - d // 2],
            send_sem=zos.at[s, a, d // 2], recv_sem=zor.at[s, a, 1 - d // 2],
            device_id={"height": z + d - 1},
        )

    def z_back(s, a, d):
        return pltpu.make_async_remote_copy(
            src_ref=zsend.at[s, a, d // 2], dst_ref=zgot.at[s, a, d // 2],
            send_sem=zos.at[s, a, d // 2], recv_sem=zor.at[s, a, d // 2],
            device_id={"height": z + d - 1},
        )

    def x_out(s, a):
        return pltpu.make_async_remote_copy(
            src_ref=xsend.at[s, a], dst_ref=xgot.at[s, a],
            send_sem=xos.at[s, a], recv_sem=xor_.at[s, a], device_id={"tm": other},
        )

    def grad_block(s, i, kind):
        pieces = []
        for j in range(2):
            kz, ki, qz, qi = key_first(kind, i, j)
            goal = total.at[s, j if kind == "queries" else i]
            weight = probs[s, i, j] * jnp.exp2(row(block_stats.at[s, i, j], 0) - row(goal, 0))
            ds = (weight * (dws[s, i, j] - row(goal, 1))).astype(bf)
            dv = jnp.dot(weight.astype(bf), qz[s, 1, qi], preferred_element_type=f32)
            dk = jnp.dot(ds, qz[s, 0, qi], preferred_element_type=f32)
            dq = lax.dot_general(
                kz[s, 0, ki], ds, (((0,), (0,)), ((), ())), preferred_element_type=f32
            )
            pieces.append((dk, dv, dq))
        if kind == "queries":
            for j in range(2):
                qacc[j] += pieces[j][2]
            done = ((pieces[0][0] + pieces[1][0]) * scale, pieces[0][1] + pieces[1][1])
            places = (1, 2)
        else:
            for j in range(2):
                kacc[j] += pieces[j][0]
                vacc[j] += pieces[j][1]
            done = ((pieces[0][2] + pieces[1][2]).T * scale,)
            places = (0,)

        @pl.when(i == 1)
        def _():
            for value, place in zip(done, places):
                fin[s, place] = value

        @pl.when(i != 1)
        def _():
            for a, value in enumerate(done):
                zsend[s, a, i // 2] = value.astype(bf)
                z_out(s, a, i).start()

    def grads(s, first, last, centre_first=False):
        def action(s, kind):
            if first == 0:
                if kind == "queries":
                    qacc[...] = jnp.zeros_like(qacc)
                else:
                    kacc[...] = jnp.zeros_like(kacc)
                    vacc[...] = jnp.zeros_like(vacc)

            @pl.loop(first, last)
            def _(turn):
                i = lax.rem((1 if centre_first else 0) + 2 * turn, 3)

                @pl.when(live(i))
                def _():
                    grad_block(s, i, kind)

            if last < 3:
                return
            if kind == "queries":
                xsend[s, 0] = (qacc[1].T * scale).astype(bf)
                x_out(s, 0).start()
                fin[s, 0] = qacc[0].T * scale
            else:
                xsend[s, 0] = (kacc[1] * scale).astype(bf)
                x_out(s, 0).start()
                xsend[s, 1] = vacc[1].astype(bf)
                if s > 0:
                    x_out(s, 1).start()
                fin[s, 1] = kacc[0] * scale
                fin[s, 2] = vacc[0]
        each(s, action)

    def late_x_out(s):
        def action(s, kind):
            if kind == "keys":
                x_out(s, 1).start()
        each(s, action)

    outs = (q_out, k_out, v_out)

    def finish(s):
        def action(s, kind):
            z_places, x_places = ((1, 2), (0,)) if kind == "queries" else ((0,), (1, 2))
            for a, place in enumerate(z_places):
                for d in (0, 2):
                    @pl.when(live(d))
                    def _():
                        z_back(s, a, d).wait_recv()
                        fin[s, place] += zgot[s, a, d // 2].astype(f32)
                outs[place][s] = fin[s, place].astype(bf)
            for a, place in enumerate(x_places):
                x_out(s, a).wait_recv()
                outs[place][s] = (fin[s, place] + xgot[s, a].astype(f32)).astype(bf)
        each(s, action)

    def drain(s):
        def action(s, kind):
            for a in range(2):
                x_in(s, a, kind).wait_send()
                for d in (0, 2):
                    @pl.when(live(d))
                    def _():
                        z_in(s, a, d, kind).wait_send()
            if kind == "queries":
                for j in range(2):
                    x_stat(s, j).wait_send()
            else:
                for_z_stats(lambda i, r: z_stat(s, i, r).wait_send())
            z_n, x_n = (2, 1) if kind == "queries" else (1, 2)
            for a in range(z_n):
                for d in (0, 2):
                    @pl.when(live(d))
                    def _():
                        z_out(s, a, d).wait_send()
            for a in range(x_n):
                x_out(s, a).wait_send()
        each(s, action)

    send_in(0, 0)
    send_in(0, 1)
    send_in(1, 0)
    for s in range(slots):
        own_part(s)
    far_part(0, (0,))
    far_part(0, (1,))
    send_stats(0)
    send_in(1, 1)
    send_in(2, 0)
    far_part(1, (0,))
    take_stats(0)
    grads(0, 0, 1, True)
    far_part(1, (1,))
    send_stats(1)
    send_in(2, 1)
    grads(0, 1, 3, True)
    take_stats(1)
    grads(1, 0, 1)
    far_part(2, (0, 1))
    send_stats(2)
    late_x_out(0)
    grads(1, 1, 3)
    take_stats(2)
    grads(2, 0, 3)
    for s in range(slots):
        finish(s)
    for s in range(slots):
        drain(s)


def settle_kernel(a_in, b_in, c_in, a_out, b_out, c_out, sems):
    pairs = ((a_in, a_out), (b_in, b_out), (c_in, c_out))
    copies = [pltpu.make_async_copy(src, dst, sems.at[i]) for i, (src, dst) in enumerate(pairs)]
    for copy in copies:
        copy.start()
    for copy in copies:
        copy.wait()


def banded(query_in, key_in, value_in, out_grad):
    head_count, frames, rows, cols, depth = query_in.shape
    assert cols == 2 * TILE_C
    tokens = frames * rows * cols
    flat = (head_count, tokens, depth)
    slots = head_count
    bf, f32 = jnp.bfloat16, jnp.float32
    dma = pltpu.SemaphoreType.DMA
    outs = pl.pallas_call(
        banded_kernel,
        out_shape=[pltpu.VMEM(flat, bf)] * 3,
        in_specs=[pl.BlockSpec(memory_space=pl.ANY)] * 4,
        out_specs=[pl.BlockSpec(memory_space=pltpu.VMEM)] * 3,
        scratch_shapes=[
            pltpu.VMEM((slots, 2, 3, tokens, depth), bf),
            pltpu.VMEM((slots, 2, 2, tokens, depth), bf),
            pltpu.VMEM((slots, 3, 2, tokens, tokens), f32),
            pltpu.VMEM((slots, 3, 2, tokens, tokens), f32),
            pltpu.VMEM((slots, 3, 2, 8, tokens), f32),
            pltpu.VMEM((slots, 3, tokens // 64, 128), f32),
            pltpu.VMEM((slots, 3, 3, tokens // 64, 128), f32),
            pltpu.VMEM((slots, 3, 8, tokens), f32),
            pltpu.VMEM((slots, 3, tokens, depth), f32),
            pltpu.VMEM((2, tokens, depth), f32),
            pltpu.VMEM((2, tokens, depth), f32),
            pltpu.VMEM((2, depth, tokens), f32),
            pltpu.VMEM((slots, 2, 2, tokens, depth), bf),
            pltpu.VMEM((slots, 2, tokens, depth), bf),
            pltpu.VMEM((slots, 2, 2, tokens, depth), bf),
            pltpu.VMEM((slots, 2, tokens, depth), bf),
            dma((slots, 2, 2)),
            dma((slots, 2)),
            dma((slots, 2)),
            dma((slots, 2, 3)),
            dma((slots, 2, 3)),
            dma((slots, 3, 3)),
            dma((slots, 3, 3)),
            dma((slots, 2)),
            dma((slots, 2)),
            dma((slots, 2, 2)),
            dma((slots, 2, 2)),
        ],
        compiler_params=pltpu.CompilerParams(
            collective_id=0, has_side_effects=True, vmem_limit_bytes=60 * 1024 * 1024
        ),
    )(*(a.reshape(flat) for a in (query_in, key_in, value_in, out_grad)))
    outs = pl.pallas_call(
        settle_kernel,
        out_shape=[jax.ShapeDtypeStruct(flat, bf)] * 3,
        in_specs=[pl.BlockSpec(memory_space=pl.ANY)] * 3,
        out_specs=[pl.BlockSpec(memory_space=pl.ANY)] * 3,
        scratch_shapes=[dma((3,))],
    )(*(pltpu.with_memory_space_constraint(o, pltpu.VMEM) for o in outs))
    return tuple(o.reshape(query_in.shape) for o in outs)


def solution(mesh):
    return jax.shard_map(
        banded if mesh.shape["tm"] == 2 else local,
        mesh=mesh,
        in_specs=(
            P("head", "tm", "height", None, None),
            P("head", "tm", "height", None, None),
            P("head", "tm", "height", None, None),
            P("head", "tm", "height", None, None),
        ),
        out_specs=(
            P("head", "tm", "height", None, None),
            P("head", "tm", "height", None, None),
            P("head", "tm", "height", None, None),
        ),
        check_vma=False,
    )
```

```python
import jax
import jax.numpy as jnp
from jax import lax
from jax.experimental import pallas as pl
from jax.experimental.pallas import tpu as pltpu
from jax.sharding import PartitionSpec as P

TILE_C = 8


def shifted(block, axis, distance):
    devices = range(lax.axis_size(axis))
    route = [(i - distance, i) for i in devices if i - distance in devices]
    return lax.ppermute(block, axis, route)


def shortened(x):
    return jax.tree.map(lambda a: a.astype(jnp.bfloat16) if a.dtype == jnp.float32 else a, x)


def extended(x, sides, width):
    for axis, dim in sides:
        size, length = (lax.axis_size(axis), x.shape[dim])
        up = [(i, (i + 1) % size) for i in range(size - 1)]
        down = [(j, i) for i, j in up]
        last = lax.slice_in_dim(x, length - width, length, axis=dim)
        first = lax.slice_in_dim(x, 0, width, axis=dim)
        before = lax.ppermute(last, axis, up)
        after = lax.ppermute(first, axis, down)
        x = jnp.concatenate([before, x, after], axis=dim)
    return x


def neighbour_live():
    offsets = jnp.arange(3, dtype=jnp.int32) - 1
    frame_pos = lax.axis_index("tm") + offsets
    row_pos = lax.axis_index("height") + offsets
    frame_ok = (frame_pos >= 0) & (frame_pos < lax.axis_size("tm"))
    row_ok = (row_pos >= 0) & (row_pos < lax.axis_size("height"))
    return frame_ok[:, None] & row_ok[None, :]


def span_live(neighbour_ok, tile_index, span_start, frame_count, row_count, span_width, col_tile):
    columns = span_start + jnp.arange(span_width, dtype=jnp.int32)
    near_cols = jnp.abs(columns // col_tile - tile_index) <= 1
    live_mask = neighbour_ok[:, :, None, None, None] & near_cols[None, None, None, None, :]
    return jnp.broadcast_to(live_mask, (3, 3, frame_count, row_count, span_width)).reshape(-1)


def scores_of(left_rows, right_rows, live_mask, score_scale):
    raw_scores = (
        jnp.einsum("hqd,hkd->hqk", left_rows, right_rows, preferred_element_type=jnp.float32)
        * score_scale
    )
    return jnp.where(live_mask, raw_scores, -jnp.inf)


def whole_span(array, span_start, span_size, axis_pos):
    return isinstance(span_start, int) and span_start == 0 and (span_size == array.shape[axis_pos])


def cut_span(array, span_start, span_size, axis_pos):
    if whole_span(array, span_start, span_size, axis_pos):
        return array
    return lax.dynamic_slice_in_dim(array, jnp.asarray(span_start, jnp.int32), span_size, axis_pos)


def add_span(array, piece):
    return array + piece


def run_tiles(tile_step, tile_count, col_tile, carried):
    edge_width = 2 * col_tile
    carried = tile_step(0, 0, edge_width, carried)
    return tile_step(tile_count - 1, (tile_count - 2) * col_tile, edge_width, carried)


def send_rows(parts, offset):
    return (
        shifted(parts[0].astype(jnp.bfloat16), "height", offset).astype(jnp.float32),
        shifted(parts[1].astype(jnp.bfloat16), "height", offset).astype(jnp.float32),
    )


def send_frames(parts, offset):
    return shifted((shortened(parts[0]), shortened(parts[1])), "tm", offset)


def local(query_in, key_in, value_in, out_grad):
    head_count, frame_count, row_count, col_count, head_depth = query_in.shape
    col_tile = TILE_C
    tile_count = col_count // col_tile
    score_scale = head_depth ** (-0.5)
    spread_shape = (head_count, 1, 1, frame_count, row_count, col_count, head_depth)
    ext_shape = (head_count, 3, 3, frame_count, row_count, col_count, head_depth)
    stat_shape = (head_count, frame_count, row_count, col_tile)
    neighbour_ok = neighbour_live()
    keys_ext, values_ext = (
        extended(key_in.reshape(spread_shape), (("tm", 1), ("height", 2)), 1),
        extended(value_in.reshape(spread_shape), (("tm", 1), ("height", 2)), 1),
    )

    def query_step(tile_index, span_start, span_width, carried):
        grad_q, row_totals, row_deltas, grad_k, grad_v = carried
        own_start = jnp.asarray(tile_index * col_tile, jnp.int32)
        q_rows = cut_span(query_in, own_start, col_tile, 3).reshape(head_count, -1, head_depth)
        g_rows = cut_span(out_grad, own_start, col_tile, 3).reshape(head_count, -1, head_depth)
        k_span = cut_span(keys_ext, span_start, span_width, 5).reshape(head_count, -1, head_depth)
        v_span = cut_span(values_ext, span_start, span_width, 5).reshape(head_count, -1, head_depth)
        live_mask = span_live(
            neighbour_ok, tile_index, span_start, frame_count, row_count, span_width, col_tile
        )
        scores = scores_of(q_rows, k_span, live_mask[None, None, :], score_scale)
        row_max = jnp.max(scores, axis=-1, keepdims=True)
        log_total = row_max + jnp.log(jnp.sum(jnp.exp(scores - row_max), axis=-1, keepdims=True))
        weights = jnp.exp(scores - log_total)
        weight_bf = weights.astype(jnp.bfloat16)
        attended = jnp.einsum("hqk,hkd->hqd", weight_bf, v_span, preferred_element_type=jnp.float32)
        row_delta = jnp.sum(g_rows.astype(jnp.float32) * attended, axis=-1, keepdims=True)
        d_weights = jnp.einsum("hqd,hkd->hqk", g_rows, v_span, preferred_element_type=jnp.float32)
        d_scores = (weights * (d_weights - row_delta)).astype(jnp.bfloat16)
        grad_piece = (
            jnp.einsum("hqk,hkd->hqd", d_scores, k_span, preferred_element_type=jnp.float32)
            * score_scale
        )
        grad_q = lax.dynamic_update_slice_in_dim(
            grad_q, grad_piece.reshape(stat_shape + (head_depth,)), own_start, 3
        )
        row_totals = lax.dynamic_update_slice_in_dim(
            row_totals, log_total.reshape(stat_shape), own_start, 3
        )
        row_deltas = lax.dynamic_update_slice_in_dim(
            row_deltas, row_delta.reshape(stat_shape), own_start, 3
        )
        span_shape = (head_count, 3, 3, frame_count, row_count, span_width, head_depth)
        key_piece = (
            jnp.einsum("hqk,hqd->hkd", d_scores, q_rows, preferred_element_type=jnp.float32)
            * score_scale
        )
        value_piece = jnp.einsum(
            "hqk,hqd->hkd", weight_bf, g_rows, preferred_element_type=jnp.float32
        )
        grad_k = add_span(grad_k, key_piece.reshape(span_shape))
        grad_v = add_span(grad_v, value_piece.reshape(span_shape))
        return (grad_q, row_totals, row_deltas, grad_k, grad_v)

    stat_full = (head_count, frame_count, row_count, col_count)
    initial = (
        jnp.zeros(query_in.shape, jnp.float32),
        jnp.zeros(stat_full, jnp.float32),
        jnp.zeros(stat_full, jnp.float32),
        jnp.zeros(ext_shape, jnp.float32),
        jnp.zeros(ext_shape, jnp.float32),
    )
    grad_q, row_totals, row_deltas, grad_k, grad_v = run_tiles(
        query_step, tile_count, col_tile, initial
    )
    query_grad = grad_q.astype(jnp.bfloat16)
    from_above = send_rows((grad_k[:, :, 0], grad_v[:, :, 0]), -1)
    from_below = send_rows((grad_k[:, :, 2], grad_v[:, :, 2]), 1)
    part_k = grad_k[:, :, 1] + from_above[0] + from_below[0]
    part_v = grad_v[:, :, 1] + from_above[1] + from_below[1]
    from_next = send_frames((part_k[:, 0], part_v[:, 0]), -1)
    from_prev = send_frames((part_k[:, 2], part_v[:, 2]), 1)
    key_total = part_k[:, 1] + from_next[0] + from_prev[0]
    value_total = part_v[:, 1] + from_next[1] + from_prev[1]
    return (query_grad, key_total.astype(jnp.bfloat16), value_total.astype(jnp.bfloat16))


LOG2_E = 1.4426950408889634


def job_kinds(slot, slots):
    return ("keys" if slot < slots - slots // 2 else "queries", "keys" if slot < slots // 2 else "queries")


def banded_kernel(
    q_in, k_in, v_in, g_in, q_out, k_out, v_out,
    zb, xb, probs, dws, block_stats, sloc, sfar, total, fin, kacc, vacc, qacc,
    zsend, xsend, zgot, xgot,
    loc, xis, xir, zis, zir, ss, sr, xos, xor_, zos, zor,
):
    slots, tokens, depth = q_in.shape
    scale = depth ** (-0.5)
    rate = scale * LOG2_E
    f32, bf = jnp.float32, jnp.bfloat16
    x = lax.axis_index("tm")
    z = lax.axis_index("height")
    z_count = lax.axis_size("height")
    parity = lax.rem(lax.axis_index("head"), 2)
    other = 1 - x

    def at_z(distance):
        return (z + distance >= 0) & (z + distance < z_count)

    def live(i):
        return at_z(i - 1)

    def each(s, action):
        kinds = job_kinds(s, slots)
        if kinds[0] == kinds[1]:
            action(s, kinds[0])
        else:
            for p in range(2):
                @pl.when(parity == p)
                def _():
                    action(s, kinds[p])

    def x_side(kind):
        return (q_in, g_in) if kind == "queries" else (k_in, v_in)

    def z_side(kind):
        return (k_in, v_in) if kind == "queries" else (q_in, g_in)

    def key_first(kind, i, j):
        return (zb, i, xb, j) if kind == "queries" else (xb, j, zb, i)

    groups = tokens // 128
    nothing = jnp.concatenate(
        [jnp.full((groups, 128), -jnp.inf, f32), jnp.zeros((groups, 128), f32)], axis=0
    )
    block_stats[:, :, :, 0:1, :] = jnp.full((slots, 3, 2, 1, tokens), -jnp.inf, f32)
    block_stats[:, :, :, 1:8, :] = jnp.zeros((slots, 3, 2, 7, tokens), f32)
    sfar[...] = jnp.broadcast_to(nothing, sfar.shape)

    def own_copies(s, a, kind):
        return [
            pltpu.make_async_copy(x_side(kind)[a].at[s], xb.at[s, a, 0], loc.at[s, a, 0]),
            pltpu.make_async_copy(z_side(kind)[a].at[s], zb.at[s, a, 1], loc.at[s, a, 1]),
        ]

    def start_own(s, kind):
        for a in range(2):
            for copy in own_copies(s, a, kind):
                copy.start()

    barrier = pltpu.get_barrier_semaphore()
    pl.semaphore_signal(barrier, inc=1, device_id={"tm": other})
    for distance in (-1, 1):
        @pl.when(at_z(distance))
        def _():
            pl.semaphore_signal(barrier, inc=1, device_id={"height": z + distance})
    for s in range(slots):
        each(s, start_own)
    pl.semaphore_wait(barrier, 1 + sum(jnp.where(at_z(n), 1, 0) for n in (-1, 1)))

    def x_in(s, a, kind):
        return pltpu.make_async_remote_copy(
            src_ref=x_side(kind)[a].at[s], dst_ref=xb.at[s, a, 1],
            send_sem=xis.at[s, a], recv_sem=xir.at[s, a], device_id={"tm": other},
        )

    def z_in(s, a, d, kind):
        return pltpu.make_async_remote_copy(
            src_ref=z_side(kind)[a].at[s], dst_ref=zb.at[s, a, 2 - d],
            send_sem=zis.at[s, a, d], recv_sem=zir.at[s, a, 2 - d], device_id={"height": z + d - 1},
        )

    def z_arrived(s, a, i, kind):
        return pltpu.make_async_remote_copy(
            src_ref=z_side(kind)[a].at[s], dst_ref=zb.at[s, a, i],
            send_sem=zis.at[s, a, 0], recv_sem=zir.at[s, a, i], device_id={"height": z + i - 1},
        )

    def send_in(s, a):
        def action(s, kind):
            x_in(s, a, kind).start()
            for d in (0, 2):
                @pl.when(live(d))
                def _():
                    z_in(s, a, d, kind).start()
        each(s, action)

    def folded(block):
        return block.reshape(tokens // 8, 8, tokens)

    def row(ref, n):
        return ref[n:n + 1, :]

    def product(s, a, i, j, kind):
        kz, ki, qz, qi = key_first(kind, i, j)
        return lax.dot_general(
            kz[s, a, ki], qz[s, a, qi], (((1,), (1,)), ((), ())), preferred_element_type=f32
        )

    def column(op, block):
        return op(op(folded(block), axis=0), axis=0, keepdims=True)

    def blocks(s, i, columns, kind, arrays):
        raws = [product(s, 0, i, j, kind) for j in columns] if 0 in arrays else None
        slopes = [product(s, 1, i, j, kind) for j in columns] if 1 in arrays else None
        for n, j in enumerate(columns):
            out = block_stats.at[s, i, j]
            if raws:
                top = column(jnp.max, raws[n])
                prob = jnp.exp2((raws[n] - top) * rate)
                probs[s, i, j] = prob
                out[0:1, :] = top * rate
                out[1:2, :] = column(jnp.sum, prob)
            else:
                prob = probs[s, i, j]
            if slopes:
                dws[s, i, j] = slopes[n]
                out[2:3, :] = column(jnp.sum, prob * slopes[n])

    def own_part(s):
        def action(s, kind):
            for a in range(2):
                for copy in own_copies(s, a, kind):
                    copy.wait()
            blocks(s, 1, (0,), kind, (0, 1))
        each(s, action)

    def far_part(s, arrays):
        def action(s, kind):
            for a in arrays:
                x_in(s, a, kind).wait_recv()
            blocks(s, 1, (1,), kind, arrays)

            @pl.loop(0, 2)
            def _(turn):
                i = 2 * turn

                @pl.when(live(i))
                def _():
                    for a in arrays:
                        z_arrived(s, a, i, kind).wait_recv()
                    blocks(s, i, (0, 1), kind, arrays)
        each(s, action)

    def weighed(tops, pairs):
        top = tops[0]
        for t in tops[1:]:
            top = jnp.maximum(top, t)
        factors = [jnp.exp2(t - top) for t in tops]
        mass = sum(f * m for f, (m, _) in zip(factors, pairs))
        pull = sum(f * d for f, (_, d) in zip(factors, pairs))
        return top + jnp.log(mass) * LOG2_E, pull / mass

    def merge_blocks(s, b, parts):
        tops = [row(p, 0) for p in parts]
        pairs = [(row(p, 1), row(p, 2)) for p in parts]
        for n, value in enumerate(weighed(tops, pairs)):
            for g in range(groups):
                r = n * groups + g
                sloc[s, b, r:r + 1, :] = value[:, g * 128:(g + 1) * 128]

    def merge_devices(s, b, far):
        parts = [ref[...] for ref in [sloc.at[s, b]] + far]
        level, delta = weighed(
            [p[:groups] for p in parts], [(1.0, p[groups:]) for p in parts]
        )
        for n, value in enumerate((level, delta)):
            for g in range(groups):
                total[s, b, n:n + 1, g * 128:(g + 1) * 128] = value[g:g + 1, :]

    def x_stat(s, j):
        return pltpu.make_async_remote_copy(
            src_ref=sloc.at[s, j], dst_ref=sfar.at[s, 1 - j, 0],
            send_sem=ss.at[s, j, 0], recv_sem=sr.at[s, 1 - j, 0], device_id={"tm": other},
        )

    def z_stat(s, i, r):
        return pltpu.make_async_remote_copy(
            src_ref=sloc.at[s, i], dst_ref=sfar.at[s, 2 - r, 2 - i],
            send_sem=ss.at[s, i, r], recv_sem=sr.at[s, 2 - r, 2 - i],
            device_id={"height": z + i + r - 2},
        )

    def z_stat_arrived(s, i, r):
        return pltpu.make_async_remote_copy(
            src_ref=sloc.at[s, i], dst_ref=sfar.at[s, i, r],
            send_sem=ss.at[s, i, r], recv_sem=sr.at[s, i, r],
            device_id={"height": z + i + r - 2},
        )

    def for_z_stats(action):
        for i in range(3):
            for r in range(3):
                if r != 2 - i:
                    @pl.when(live(i) & at_z(i + r - 2))
                    def _():
                        action(i, r)

    def send_stats(s):
        def action(s, kind):
            if kind == "queries":
                for j in (1, 0):
                    merge_blocks(s, j, [block_stats.at[s, i, j] for i in range(3)])
                    x_stat(s, j).start()
            else:
                for i in range(3):
                    @pl.when(live(i))
                    def _():
                        merge_blocks(s, i, [block_stats.at[s, i, j] for j in range(2)])
                for_z_stats(lambda i, r: z_stat(s, i, r).start())
        each(s, action)

    def take_stats(s):
        def action(s, kind):
            if kind == "queries":
                for j in range(2):
                    x_stat(s, 1 - j).wait_recv()
                    merge_devices(s, j, [sfar.at[s, j, 0]])
            else:
                for_z_stats(lambda i, r: z_stat_arrived(s, i, r).wait_recv())
                for i in range(3):
                    @pl.when(live(i))
                    def _():
                        merge_devices(s, i, [sfar.at[s, i, r] for r in range(3) if r != 2 - i])
        each(s, action)

    def z_out(s, a, d):
        return pltpu.make_async_remote_copy(
            src_ref=zsend.at[s, a, d // 2], dst_ref=zgot.at[s, a, 1 - d // 2],
            send_sem=zos.at[s, a, d // 2], recv_sem=zor.at[s, a, 1 - d // 2],
            device_id={"height": z + d - 1},
        )

    def z_back(s, a, d):
        return pltpu.make_async_remote_copy(
            src_ref=zsend.at[s, a, d // 2], dst_ref=zgot.at[s, a, d // 2],
            send_sem=zos.at[s, a, d // 2], recv_sem=zor.at[s, a, d // 2],
            device_id={"height": z + d - 1},
        )

    def x_out(s, a):
        return pltpu.make_async_remote_copy(
            src_ref=xsend.at[s, a], dst_ref=xgot.at[s, a],
            send_sem=xos.at[s, a], recv_sem=xor_.at[s, a], device_id={"tm": other},
        )

    def grad_block(s, i, kind):
        pieces = []
        for j in range(2):
            kz, ki, qz, qi = key_first(kind, i, j)
            goal = total.at[s, j if kind == "queries" else i]
            weight = probs[s, i, j] * jnp.exp2(row(block_stats.at[s, i, j], 0) - row(goal, 0))
            ds = (weight * (dws[s, i, j] - row(goal, 1))).astype(bf)
            dv = jnp.dot(weight.astype(bf), qz[s, 1, qi], preferred_element_type=f32)
            dk = jnp.dot(ds, qz[s, 0, qi], preferred_element_type=f32)
            dq = lax.dot_general(
                kz[s, 0, ki], ds, (((0,), (0,)), ((), ())), preferred_element_type=f32
            )
            pieces.append((dk, dv, dq))
        if kind == "queries":
            for j in range(2):
                qacc[j] += pieces[j][2]
            done = ((pieces[0][0] + pieces[1][0]) * scale, pieces[0][1] + pieces[1][1])
            places = (1, 2)
        else:
            for j in range(2):
                kacc[j] += pieces[j][0]
                vacc[j] += pieces[j][1]
            done = ((pieces[0][2] + pieces[1][2]).T * scale,)
            places = (0,)

        @pl.when(i == 1)
        def _():
            for value, place in zip(done, places):
                fin[s, place] = value

        @pl.when(i != 1)
        def _():
            for a, value in enumerate(done):
                zsend[s, a, i // 2] = value.astype(bf)
                z_out(s, a, i).start()

    def grads(s, first, last, centre_first=False):
        def action(s, kind):
            if first == 0:
                if kind == "queries":
                    qacc[...] = jnp.zeros_like(qacc)
                else:
                    kacc[...] = jnp.zeros_like(kacc)
                    vacc[...] = jnp.zeros_like(vacc)

            @pl.loop(first, last)
            def _(turn):
                i = lax.rem((1 if centre_first else 0) + 2 * turn, 3)

                @pl.when(live(i))
                def _():
                    grad_block(s, i, kind)

            if last < 3:
                return
            if kind == "queries":
                xsend[s, 0] = (qacc[1].T * scale).astype(bf)
                x_out(s, 0).start()
                fin[s, 0] = qacc[0].T * scale
            else:
                xsend[s, 0] = (kacc[1] * scale).astype(bf)
                x_out(s, 0).start()
                xsend[s, 1] = vacc[1].astype(bf)
                if s > 0:
                    x_out(s, 1).start()
                fin[s, 1] = kacc[0] * scale
                fin[s, 2] = vacc[0]
        each(s, action)

    def late_x_out(s):
        def action(s, kind):
            if kind == "keys":
                x_out(s, 1).start()
        each(s, action)

    outs = (q_out, k_out, v_out)

    def finish(s):
        def action(s, kind):
            z_places, x_places = ((1, 2), (0,)) if kind == "queries" else ((0,), (1, 2))
            for a, place in enumerate(z_places):
                for d in (0, 2):
                    @pl.when(live(d))
                    def _():
                        z_back(s, a, d).wait_recv()
                        fin[s, place] += zgot[s, a, d // 2].astype(f32)
                outs[place][s] = fin[s, place].astype(bf)
            for a, place in enumerate(x_places):
                x_out(s, a).wait_recv()
                outs[place][s] = (fin[s, place] + xgot[s, a].astype(f32)).astype(bf)
        each(s, action)

    def drain(s):
        def action(s, kind):
            for a in range(2):
                x_in(s, a, kind).wait_send()
                for d in (0, 2):
                    @pl.when(live(d))
                    def _():
                        z_in(s, a, d, kind).wait_send()
            if kind == "queries":
                for j in range(2):
                    x_stat(s, j).wait_send()
            else:
                for_z_stats(lambda i, r: z_stat(s, i, r).wait_send())
            z_n, x_n = (2, 1) if kind == "queries" else (1, 2)
            for a in range(z_n):
                for d in (0, 2):
                    @pl.when(live(d))
                    def _():
                        z_out(s, a, d).wait_send()
            for a in range(x_n):
                x_out(s, a).wait_send()
        each(s, action)

    send_in(0, 0)
    send_in(0, 1)
    send_in(1, 0)
    for s in range(slots):
        own_part(s)
    far_part(0, (0,))
    far_part(0, (1,))
    send_stats(0)
    send_in(1, 1)
    send_in(2, 0)
    far_part(1, (0,))
    take_stats(0)
    grads(0, 0, 1, True)
    far_part(1, (1,))
    send_stats(1)
    send_in(2, 1)
    grads(0, 1, 3, True)
    take_stats(1)
    grads(1, 0, 1)
    far_part(2, (0, 1))
    send_stats(2)
    late_x_out(0)
    grads(1, 1, 3)
    take_stats(2)
    grads(2, 0, 3)
    for s in range(slots):
        finish(s)
    for s in range(slots):
        drain(s)


def settle_kernel(a_in, b_in, c_in, a_out, b_out, c_out, sems):
    pairs = ((a_in, a_out), (b_in, b_out), (c_in, c_out))
    copies = [pltpu.make_async_copy(src, dst, sems.at[i]) for i, (src, dst) in enumerate(pairs)]
    for copy in copies:
        copy.start()
    for copy in copies:
        copy.wait()


def banded(query_in, key_in, value_in, out_grad):
    head_count, frames, rows, cols, depth = query_in.shape
    assert cols == 2 * TILE_C
    tokens = frames * rows * cols
    flat = (head_count, tokens, depth)
    slots = head_count
    bf, f32 = jnp.bfloat16, jnp.float32
    dma = pltpu.SemaphoreType.DMA
    outs = pl.pallas_call(
        banded_kernel,
        out_shape=[pltpu.VMEM(flat, bf)] * 3,
        in_specs=[pl.BlockSpec(memory_space=pl.ANY)] * 4,
        out_specs=[pl.BlockSpec(memory_space=pltpu.VMEM)] * 3,
        scratch_shapes=[
            pltpu.VMEM((slots, 2, 3, tokens, depth), bf),
            pltpu.VMEM((slots, 2, 2, tokens, depth), bf),
            pltpu.VMEM((slots, 3, 2, tokens, tokens), f32),
            pltpu.VMEM((slots, 3, 2, tokens, tokens), f32),
            pltpu.VMEM((slots, 3, 2, 8, tokens), f32),
            pltpu.VMEM((slots, 3, tokens // 64, 128), f32),
            pltpu.VMEM((slots, 3, 3, tokens // 64, 128), f32),
            pltpu.VMEM((slots, 3, 8, tokens), f32),
            pltpu.VMEM((slots, 3, tokens, depth), f32),
            pltpu.VMEM((2, tokens, depth), f32),
            pltpu.VMEM((2, tokens, depth), f32),
            pltpu.VMEM((2, depth, tokens), f32),
            pltpu.VMEM((slots, 2, 2, tokens, depth), bf),
            pltpu.VMEM((slots, 2, tokens, depth), bf),
            pltpu.VMEM((slots, 2, 2, tokens, depth), bf),
            pltpu.VMEM((slots, 2, tokens, depth), bf),
            dma((slots, 2, 2)),
            dma((slots, 2)),
            dma((slots, 2)),
            dma((slots, 2, 3)),
            dma((slots, 2, 3)),
            dma((slots, 3, 3)),
            dma((slots, 3, 3)),
            dma((slots, 2)),
            dma((slots, 2)),
            dma((slots, 2, 2)),
            dma((slots, 2, 2)),
        ],
        compiler_params=pltpu.CompilerParams(
            collective_id=0, has_side_effects=True, vmem_limit_bytes=60 * 1024 * 1024
        ),
    )(*(a.reshape(flat) for a in (query_in, key_in, value_in, out_grad)))
    outs = pl.pallas_call(
        settle_kernel,
        out_shape=[jax.ShapeDtypeStruct(flat, bf)] * 3,
        in_specs=[pl.BlockSpec(memory_space=pl.ANY)] * 3,
        out_specs=[pl.BlockSpec(memory_space=pl.ANY)] * 3,
        scratch_shapes=[dma((3,))],
    )(*(pltpu.with_memory_space_constraint(o, pltpu.VMEM) for o in outs))
    return tuple(o.reshape(query_in.shape) for o in outs)


def solution(mesh):
    return jax.shard_map(
        banded if mesh.shape["tm"] == 2 else local,
        mesh=mesh,
        in_specs=(
            P("head", "tm", "height", None, None),
            P("head", "tm", "height", None, None),
            P("head", "tm", "height", None, None),
            P("head", "tm", "height", None, None),
        ),
        out_specs=(
            P("head", "tm", "height", None, None),
            P("head", "tm", "height", None, None),
            P("head", "tm", "height", None, None),
        ),
        check_vma=False,
    )
```
